256 devices in a mesh: fsdp: 16 (over y, x_lo, core), replica: 16 (over z, x_hi).
Axes of the slice: x: 4 (x_hi: 2, x_lo: 2; x = x_hi * 2 + x_lo), y: 4, z: 8, core: 2. Of those that a mesh axis runs over, the one named last changes fastest.
Arguments:
- tokens: bfloat16 [16, 6144, 8192], P('replica', 'fsdp'), may hold values from -45 to 45
- key_grads: bfloat16 [16, 6144, 512], P('replica', 'fsdp'), may hold values from -45 to 45
- weights: float32 [16, 8192, 512], P('replica', 'fsdp'), may hold values from -6 to 6
- first_moment: float32 [16, 8192, 512], P('replica', 'fsdp'), may hold values from -4 to 4
- second_moment: float32 [16, 8192, 512], P('replica', 'fsdp'), may hold values from 0.01 to 1
- step_index: int32 [1], replicated, may hold values from 0 to 63
Outputs:
- new_weights: float32 [16, 8192, 512], P('replica', 'fsdp')
- new_first: float32 [16, 8192, 512], P('replica', 'fsdp')
- new_second: float32 [16, 8192, 512], P('replica', 'fsdp')
The draws below stay inside these ranges and needn't reach their ends.
All inputs are finite; a program needn't handle non-finite values.
Results may differ from the reference program's by a relative error of at most 0.0005.
Values may be sent and summed in bfloat16 or wider, within the bound.
No kernel may reach another device: no remote copies, remote signals or barrier semaphores. Data moves between devices by JAX's collectives and lax.ppermute only.
A program may use at most 128 MiB of HBM per device.

```python
import math
import jax
import jax.numpy as jnp
from jax import lax

D = 8192
KVC = 512
REPLICAS = 16
TOKENS_R = 6144
LEVELS = 4


def draw_tokens(key, part):
    key_scale, key_base = jax.random.split(jax.random.fold_in(key, 11), 2)
    position = jnp.arange(D, dtype=jnp.float32) / D
    jitter = jax.random.uniform(key_scale, (D,), jnp.float32)
    column_scale = 10.0 ** (0.5 * position + 0.5 * jitter)
    values = jax.random.truncated_normal(key_base, -4.0, 4.0, (REPLICAS, TOKENS_R, D), jnp.float32)
    return (values * column_scale).astype(jnp.bfloat16)


def draw_key_grads(key, part):
    key_scale, key_base = jax.random.split(jax.random.fold_in(key, 23), 2)
    jitter = jax.random.uniform(key_scale, (KVC,), jnp.float32)
    column_scale = 10.0 ** jitter
    values = jax.random.truncated_normal(key_base, -4.0, 4.0, (REPLICAS, TOKENS_R, KVC), jnp.float32)
    return (values * column_scale).astype(jnp.bfloat16)


def level_of(key, extent, pieces, smallest, largest):
    def one(dim, parts):
        draws = jax.random.uniform(jax.random.fold_in(jax.random.fold_in(key, 6), dim), (parts,), jnp.float32, smallest / len(pieces), largest / len(pieces))
        return jnp.repeat(jnp.exp(draws), extent[dim] // parts).reshape((-1,) + (1,) * (len(extent) - dim - 1))

    factor_of = one(*pieces[0])
    for cut in pieces[1:]:
        factor_of = factor_of * one(*cut)
    return factor_of


def normal_values(key, shape, spread, bound, cuts=(), kind=jnp.bfloat16):
    result = spread * jax.random.normal(key, shape, jnp.float32)
    if cuts:
        result = result * level_of(key, shape, cuts, -0.22, 0.18)
    return jnp.clip(result, -bound, bound).astype(kind)


def setup_inputs(seed: int = 0) -> dict:
    streams_of = jax.random.split(jax.random.key(seed), 7)
    return {
        "tokens": draw_tokens(jax.random.fold_in(streams_of[6], 71), 0),
        "key_grads": draw_key_grads(jax.random.fold_in(streams_of[6], 71), 0),
        "weights": normal_values(streams_of[2], (REPLICAS, D, KVC), 1.0, 6.0, ((0, 16), (1, 16)), jnp.float32),
        "first_moment": normal_values(streams_of[3], (REPLICAS, D, KVC), 0.5, 4.0, ((0, 16), (1, 16)), jnp.float32),
        "second_moment": jnp.clip(jnp.exp(math.log(1.0) - 4.6051702 * jax.random.uniform(streams_of[4], (REPLICAS, D, KVC), jnp.float32) ** level_of(streams_of[4], (REPLICAS, D, KVC), ((0, 16), (1, 16)), -0.2, 0.2)), 0.01, 1.0),
        "step_index": jax.random.randint(streams_of[5], (1,), 0, 64).astype(jnp.int32),
    }


BETA_ONE = 0.9
BETA_TWO = 0.95
LEARN_RATE = 0.08
ADAM_EPS = 1e-08
NORM_EPS = 1e-06

def one_replica(operands):
    inputs, grads_out = operands
    return jnp.dot(inputs.T, grads_out, preferred_element_type=jnp.float32)

def reference(tokens, key_grads, weights, first_moment, second_moment, step_index):
    gradient = lax.map(one_replica, (tokens, key_grads))
    squares = lax.optimization_barrier(jnp.sum(gradient * gradient, axis=(1, 2), keepdims=True))
    grad_norm = jnp.sqrt(squares)
    clip_factor = jnp.minimum(1.0, math.sqrt(D * KVC) / (grad_norm + NORM_EPS))
    clipped = clip_factor * gradient
    new_first = BETA_ONE * first_moment + (1.0 - BETA_ONE) * clipped
    new_second = BETA_TWO * second_moment + (1.0 - BETA_TWO) * clipped * clipped
    step_count = (step_index[0] + 1).astype(jnp.float32)
    first_fix = 1.0 - jnp.power(BETA_ONE, step_count)
    second_fix = 1.0 - jnp.power(BETA_TWO, step_count)
    change = LEARN_RATE * (new_first / first_fix) / (jnp.sqrt(new_second / second_fix) + ADAM_EPS)
    updated = weights - change
    replica_ids = jnp.arange(REPLICAS, dtype=jnp.int32)
    distance = jnp.power(jnp.int32(2), (step_index[0] % LEVELS).astype(jnp.int32)).astype(jnp.int32)
    partner = jnp.where(replica_ids // distance % 2 == 0, replica_ids + distance, replica_ids - distance).astype(jnp.int32)
    new_weights = 0.5 * (updated + jnp.take(updated, partner, axis=0))
    return (new_weights, new_first, new_second)
```

```python
from functools import partial
import math

import jax
import jax.numpy as jnp
from jax import lax
from jax.experimental import pallas as pl
from jax.experimental.pallas import tpu as pltpu
from jax.sharding import PartitionSpec as P

BETA_ONE = 0.9
BETA_TWO = 0.95
LEARN_RATE = 0.08
ADAM_EPS = 1e-08
NORM_EPS = 1e-06

SEND_SCALE = 2.0**-8
RAISE = 2.0**8

X, A, B = 1, 2, 4
PARTS = ((0, 176, (X, A, B)), (176, 176, (A, B, X)), (352, 160, (B, X, A)))


def neighbour(i, dim):
    y, x, c = i >> 2, (i >> 1) & 1, i & 1
    g = y ^ (y >> 1)
    if dim == X:
        x ^= 1
    elif dim == A:
        g ^= 1
    elif dim == B:
        g ^= 2
    else:
        c ^= 1
    y = g ^ (g >> 1)
    return (y << 2) | (x << 1) | c


def exchange(array, dim):
    return lax.ppermute(array, "fsdp", [(i, neighbour(i, dim)) for i in range(16)])


def from_partner(apart, array):
    return lax.ppermute(array, "replica", [(i, i ^ 1 << apart) for i in range(16)])


def block_of(me, d, flip):
    y, x, c = me >> 2, (me >> 1) & 1, me & 1
    g = (y ^ (y >> 1)) ^ (d >> 1)
    return ((g ^ (g >> 1)) << 2) | ((x ^ (d & 1)) << 1) | (c ^ flip)


def far(j):
    return 7 ^ ((1 << j) & 7)


def near(j):
    return (1 << j) & 7


FAR = [far(j) for j in range(4)]
NEAR = [near(j) for j in range(4)]


def gather_kernel(me, tokens, out):
    out[...] = tokens[...]


def gather(me, tokens, order):
    t = tokens.shape[0]
    return pl.pallas_call(
        gather_kernel,
        grid_spec=pltpu.PrefetchScalarGridSpec(
            num_scalar_prefetch=1,
            grid=(4,),
            in_specs=[pl.BlockSpec((t, 512), lambda j, me: (0, block_of(me[0], order(j), 1)))],
            out_specs=pl.BlockSpec((t, 512), lambda j, me: (0, j)),
        ),
        out_shape=jax.ShapeDtypeStruct((t, 2048), tokens.dtype),
        cost_estimate=pl.CostEstimate(flops=0, bytes_accessed=4 * t * 2048, transcendentals=0),
        name="gather",
    )(me, tokens)


def product_kernel(me, mine, theirs, g_mine, g_theirs, out):
    dims = (((0,), (0,)), ((), ()))
    out[0] = lax.dot_general(
        mine[...], g_mine[...], dims, preferred_element_type=jnp.float32
    ) + lax.dot_general(theirs[...], g_theirs[...], dims, preferred_element_type=jnp.float32)


def product(me, mine, theirs, g_mine, g_theirs, order):
    t, k = g_mine.shape
    return pl.pallas_call(
        product_kernel,
        grid_spec=pltpu.PrefetchScalarGridSpec(
            num_scalar_prefetch=1,
            grid=(4,),
            in_specs=[
                pl.BlockSpec((t, 512), lambda j, me: (0, block_of(me[0], order(j), 0))),
                pl.BlockSpec((t, 512), lambda j, me: (0, j)),
                pl.BlockSpec((t, k), lambda j, me: (0, 0)),
                pl.BlockSpec((t, k), lambda j, me: (0, 0)),
            ],
            out_specs=pl.BlockSpec((1, 512, k), lambda j, me: (j, 0, 0)),
        ),
        out_shape=jax.ShapeDtypeStruct((4, 512, k), jnp.float32),
        cost_estimate=pl.CostEstimate(
            flops=2 * 2 * t * 2048 * k, bytes_accessed=4 * t * 2048 + 16 * 512 * k, transcendentals=0
        ),
        name="product",
    )(me, mine, theirs, g_mine, g_theirs)


def local(tokens, key_grads, weights, first_moment, second_moment, step_index):
    inputs = tokens[0]
    grads_out = key_grads[0]
    step_bit = step_index[0] % 4
    me = lax.axis_index("fsdp")[None]

    g_theirs = exchange(grads_out, 0)
    theirs_far = exchange(gather(me, inputs, far), 0)
    theirs_near = exchange(gather(me, inputs, near), 0)
    acc_far = product(me, inputs, theirs_far, grads_out, g_theirs, far)
    acc_near = product(me, inputs, theirs_near, grads_out, g_theirs, near)

    def own(d, row, rows):
        source, slot = (acc_far, FAR.index(d)) if d in FAR else (acc_near, NEAR.index(d))
        return source[slot, row : row + rows] * SEND_SCALE

    def pack(*blocks):
        return jnp.stack(blocks).astype(jnp.float16)

    first = [
        exchange(pack(own(e1 | e2, r, n), own(7, r, n)), e1) for r, n, (e1, e2, e3) in PARTS
    ]
    second = [exchange(pack(own(e1, r, n), own(e1 | e3, r, n)), e1) for r, n, (e1, e2, e3) in PARTS]
    f32 = jnp.float32
    third = [
        exchange(
            pack(own(e2, r, n) + one[0].astype(f32), own(e2 | e3, r, n) + one[1].astype(f32)), e2
        )
        for (r, n, (e1, e2, e3)), one in zip(PARTS, first)
    ]
    fourth = [
        exchange(pack(own(e3, r, n) + two[1].astype(f32) + three[1].astype(f32)), e3)
        for (r, n, (e1, e2, e3)), two, three in zip(PARTS, second, third)
    ]
    pieces = [
        own(0, r, n) + two[0].astype(f32) + three[0].astype(f32) + four[0].astype(f32)
        for (r, n, _), two, three, four in zip(PARTS, second, third, fourth)
    ]
    gradient = jnp.concatenate(pieces, axis=0) * RAISE

    squares = jnp.sum(gradient * gradient).reshape(1, 1)
    pair = [(i, i ^ 1) for i in range(16)]
    for moves in (
        (lambda i: i ^ 1, lambda i: i ^ 2, lambda i: i ^ 3),
        (lambda i: (i + 4) % 16, lambda i: (i + 8) % 16, lambda i: (i + 12) % 16),
    ):
        squares = squares + sum(
            lax.ppermute(squares, "fsdp", [(i, move(i)) for i in range(16)]) for move in moves
        )
    grad_norm = jnp.sqrt(squares[0, 0])
    clip_factor = jnp.minimum(1.0, math.sqrt(8192 * 512) / (grad_norm + NORM_EPS))
    clipped = clip_factor * gradient
    new_first = BETA_ONE * first_moment[0] + (1.0 - BETA_ONE) * clipped
    new_second = BETA_TWO * second_moment[0] + (1.0 - BETA_TWO) * clipped * clipped
    step_count = (step_index[0] + 1).astype(jnp.float32)
    first_fix = 1.0 - jnp.power(BETA_ONE, step_count)
    second_fix = 1.0 - jnp.power(BETA_TWO, step_count)
    change = LEARN_RATE * (new_first / first_fix) / (jnp.sqrt(new_second / second_fix) + ADAM_EPS)
    updated = weights[0] - change
    branches = [partial(from_partner, apart) for apart in range(4)]
    theirs = lax.switch(step_bit, branches, updated.astype(jnp.float16))
    new_weights = 0.5 * (updated + theirs.astype(jnp.float32))
    return (new_weights[None], new_first[None], new_second[None])


def solution(mesh):
    spec = P("replica", "fsdp", None)
    return jax.shard_map(
        local,
        mesh=mesh,
        in_specs=(spec, spec, spec, spec, spec, P()),
        out_specs=(spec, spec, spec),
        check_vma=False,
    )
```

```python
from functools import partial
import math

import jax
import jax.numpy as jnp
from jax import lax
from jax.experimental import pallas as pl
from jax.experimental.pallas import tpu as pltpu
from jax.sharding import PartitionSpec as P

BETA_ONE = 0.9
BETA_TWO = 0.95
LEARN_RATE = 0.08
ADAM_EPS = 1e-08
NORM_EPS = 1e-06

SEND_SCALE = 2.0**-8
RAISE = 2.0**8

X, A, B = 1, 2, 4
PARTS = ((0, 176, (X, A, B)), (176, 176, (A, B, X)), (352, 160, (B, X, A)))


def neighbour(i, dim):
    y, x, c = i >> 2, (i >> 1) & 1, i & 1
    g = y ^ (y >> 1)
    if dim == X:
        x ^= 1
    elif dim == A:
        g ^= 1
    elif dim == B:
        g ^= 2
    else:
        c ^= 1
    y = g ^ (g >> 1)
    return (y << 2) | (x << 1) | c


def exchange(array, dim):
    return lax.ppermute(array, "fsdp", [(i, neighbour(i, dim)) for i in range(16)])


def from_partner(apart, array):
    return lax.ppermute(array, "replica", [(i, i ^ 1 << apart) for i in range(16)])


def block_of(me, d, flip):
    y, x, c = me >> 2, (me >> 1) & 1, me & 1
    g = (y ^ (y >> 1)) ^ (d >> 1)
    return ((g ^ (g >> 1)) << 2) | ((x ^ (d & 1)) << 1) | (c ^ flip)


def far(j):
    return 5 + j - 5 * (j // 3)


def near(j):
    return (1 << j) & 7


FAR = (5, 6, 7, 3, 5)
NEAR = (1, 2, 4, 0)
FIRST = {X: (2, (7, 3, 5)), A: (1, (6, 7, 3)), B: (0, (5, 6, 7))}
VMEM_LIMIT = 24 << 20


def fetch_kernel(wanted, me, tokens, *refs):
    *outs, sems = refs
    copies = []
    for out, (order, flip) in zip(outs, wanted):
        for j in range(4):
            column = pl.multiple_of(block_of(me[0], order(j), flip) * 512, 512)
            copies.append(
                pltpu.make_async_copy(
                    tokens.at[:, pl.ds(column, 512)],
                    out.at[:, pl.ds(j * 512, 512)],
                    sems.at[len(copies)],
                )
            )
    for copy in copies:
        copy.start()
    for copy in copies:
        copy.wait()


def fetch(me, tokens, wanted):
    t = tokens.shape[0]
    return pl.pallas_call(
        partial(fetch_kernel, wanted),
        in_specs=[
            pl.BlockSpec(memory_space=pltpu.SMEM),
            pl.BlockSpec(memory_space=pltpu.HBM),
        ],
        out_shape=[pltpu.VMEM((t, 2048), tokens.dtype)] * len(wanted),
        scratch_shapes=[pltpu.SemaphoreType.DMA((4 * len(wanted),))],
        cost_estimate=pl.CostEstimate(
            flops=0, bytes_accessed=4 * t * 2048 * len(wanted), transcendentals=0
        ),
        compiler_params=pltpu.CompilerParams(vmem_limit_bytes=VMEM_LIMIT),
        name="fetch",
    )(me, pltpu.with_memory_space_constraint(tokens, pltpu.HBM))


def hold_kernel(*refs):
    *pairs, sems = refs
    n = len(pairs) // 2
    copies = [pltpu.make_async_copy(pairs[i], pairs[n + i], sems.at[i]) for i in range(n)]
    for copy in copies:
        copy.start()
    for copy in copies:
        copy.wait()


def hold(*arrays):
    return pl.pallas_call(
        hold_kernel,
        in_specs=[pl.BlockSpec(memory_space=pltpu.HBM)] * len(arrays),
        out_shape=[pltpu.VMEM(a.shape, a.dtype) for a in arrays],
        scratch_shapes=[pltpu.SemaphoreType.DMA((len(arrays),))],
        compiler_params=pltpu.CompilerParams(vmem_limit_bytes=VMEM_LIMIT),
        name="hold",
    )(*[pltpu.with_memory_space_constraint(a, pltpu.HBM) for a in arrays])


def product_kernel(slots, mine, theirs, g_mine, g_theirs, out, tokens, grads):
    t = g_mine.shape[0]
    grads[:t] = g_mine[...]
    grads[t:] = g_theirs[...]

    def block(j, _):
        column = pl.multiple_of(j * 512, 512)
        tokens[:t] = mine[:, pl.ds(column, 512)]
        tokens[t:] = theirs[:, pl.ds(column, 512)]
        out[j] = lax.dot_general(
            tokens[...], grads[...], (((0,), (0,)), ((), ())), preferred_element_type=jnp.float32
        )
        return _

    lax.fori_loop(0, 4, block, None)
    if slots > 4:
        out[4] = out[0]


def product(mine, theirs, g_mine, g_theirs, slots):
    t, k = g_mine.shape
    vmem = pl.BlockSpec(memory_space=pltpu.VMEM)
    return pl.pallas_call(
        partial(product_kernel, slots),
        in_specs=[vmem] * 4,
        out_specs=vmem,
        scratch_shapes=[pltpu.VMEM((2 * t, 512), mine.dtype), pltpu.VMEM((2 * t, k), mine.dtype)],
        out_shape=jax.ShapeDtypeStruct((slots, 512, k), jnp.float32),
        cost_estimate=pl.CostEstimate(
            flops=2 * 2 * t * 2048 * k, bytes_accessed=4 * t * 2048 + 16 * 512 * k, transcendentals=0
        ),
        compiler_params=pltpu.CompilerParams(vmem_limit_bytes=VMEM_LIMIT),
        name="product",
    )(mine, theirs, g_mine, g_theirs)


def squares_kernel(*refs):
    *pieces, out = refs
    total = sum(jnp.sum((p[...] * p[...]).reshape(-1, 8, 512), axis=0) for p in pieces)
    total = total[:, :128] + total[:, 128:256] + total[:, 256:384] + total[:, 384:]
    total = jnp.sum(total, axis=0, keepdims=True)
    out[...] = jnp.broadcast_to(total[None], out.shape)


def squares_of(pieces):
    return pl.pallas_call(
        squares_kernel,
        out_shape=jax.ShapeDtypeStruct((16, 1, 128), jnp.float32),
        compiler_params=pltpu.CompilerParams(vmem_limit_bytes=VMEM_LIMIT),
        name="squares",
    )(*pieces)


def adam_kernel(step_index, all_squares, *refs):
    *pieces, weights, first, second, updated, clip_out = refs
    squares = jnp.sum(all_squares[...], axis=0)
    squares = jnp.sum(squares, axis=1, keepdims=True)
    norm = jnp.sqrt(squares) * RAISE
    clip = jnp.minimum(1.0, math.sqrt(8192 * 512) / (norm + NORM_EPS)) * RAISE
    clip_out[...] = jnp.broadcast_to(clip, clip_out.shape)
    steps = jnp.full((1, 1), step_index[0] + 1, jnp.int32).astype(jnp.float32)
    rate = LEARN_RATE / (1.0 - jnp.exp(steps * math.log(BETA_ONE)))
    second_scale = 1.0 / (1.0 - jnp.exp(steps * math.log(BETA_TWO)))
    row = 0
    for piece in pieces:
        rows = pl.ds(row, piece.shape[0])
        row += piece.shape[0]
        clipped = clip * piece[...]
        one = BETA_ONE * first[rows] + (1.0 - BETA_ONE) * clipped
        two = BETA_TWO * second[rows] + (1.0 - BETA_TWO) * clipped * clipped
        updated[rows] = weights[rows] - rate * one / (jnp.sqrt(two * second_scale) + ADAM_EPS)


def adam(step_index, all_squares, pieces, weights, first, second):
    vmem = pl.BlockSpec(memory_space=pltpu.VMEM)
    return pl.pallas_call(
        adam_kernel,
        in_specs=[pl.BlockSpec(memory_space=pltpu.SMEM)] + [vmem] * (len(pieces) + 4),
        out_specs=[vmem] * 2,
        out_shape=[
            jax.ShapeDtypeStruct(weights.shape, jnp.float32),
            jax.ShapeDtypeStruct((8, 512), jnp.float32),
        ],
        compiler_params=pltpu.CompilerParams(vmem_limit_bytes=VMEM_LIMIT),
        name="adam",
    )(step_index, all_squares, *pieces, weights, first, second)


def moments_kernel(clip, *refs):
    *pieces, first, second, new_first, new_second = refs
    row = 0
    for piece in pieces:
        rows = pl.ds(row, piece.shape[0])
        row += piece.shape[0]
        clipped = clip[:1] * piece[...]
        new_first[rows] = BETA_ONE * first[rows] + (1.0 - BETA_ONE) * clipped
        new_second[rows] = BETA_TWO * second[rows] + (1.0 - BETA_TWO) * clipped * clipped


def moments(clip, pieces, first, second):
    vmem = pl.BlockSpec(memory_space=pltpu.VMEM)
    return pl.pallas_call(
        moments_kernel,
        in_specs=[vmem] * (len(pieces) + 3),
        out_specs=[vmem] * 2,
        out_shape=[jax.ShapeDtypeStruct(first.shape, jnp.float32)] * 2,
        cost_estimate=pl.CostEstimate(
            flops=8 * first.size, bytes_accessed=20 * first.size, transcendentals=0
        ),
        compiler_params=pltpu.CompilerParams(vmem_limit_bytes=VMEM_LIMIT),
        name="moments",
    )(clip, *pieces, first, second)


def finish(apart, packed, updated, clip, pieces, first, second):
    theirs = from_partner(apart, packed)
    new_first, new_second = moments(clip, pieces, first, second)
    new_weights = 0.5 * (updated + theirs.astype(jnp.float32))
    return new_weights, new_first, new_second


def local(tokens, key_grads, weights, first_moment, second_moment, step_index):
    inputs = tokens[0]
    grads_out = key_grads[0]
    step_bit = step_index[0] % 4
    me, step_bit = lax.optimization_barrier((lax.axis_index("fsdp")[None], step_bit))

    g_theirs = exchange(grads_out, 0)
    (far_out,) = fetch(me, inputs, ((far, 1),))
    theirs_far = exchange(far_out, 0)
    near_out, mine_far, mine_near = fetch(me, inputs, ((near, 1), (far, 0), (near, 0)))
    theirs_near = exchange(near_out, 0)
    acc_far = product(mine_far, theirs_far, grads_out, g_theirs, 5)
    acc_near = product(mine_near, theirs_near, grads_out, g_theirs, 4)

    def own(d, row, rows):
        source, slot = (acc_far, FAR.index(d)) if d in FAR else (acc_near, NEAR.index(d))
        return source[slot, row : row + rows] * SEND_SCALE

    def pack(array):
        return array.astype(jnp.float16)

    def take(messages, which):
        return messages[which].astype(jnp.float32)

    firsts = []
    for row, rows, (e1, e2, e3) in PARTS:
        slot, order = FIRST[e1]
        message = acc_far[slot : slot + 3, row : row + rows] * SEND_SCALE
        firsts.append((exchange(pack(message), e1), order))
    packed = [pack(own(e1, row, rows)) for row, rows, (e1, e2, e3) in PARTS]
    lasts = [exchange(message, e1) for message, (_, _, (e1, _, _)) in zip(packed, PARTS)]
    acc_near, acc_far, weights, first_moment, second_moment, _ = lax.optimization_barrier(
        (acc_near, acc_far, weights[0], first_moment[0], second_moment[0], packed)
    )
    weights, first_moment, second_moment = hold(weights, first_moment, second_moment)
    acc_near, acc_far, weights, first_moment, second_moment = lax.optimization_barrier(
        (acc_near, acc_far, weights, first_moment, second_moment)
    )
    seconds = []
    for (row, rows, (e1, e2, e3)), (first, order) in zip(PARTS, firsts):
        ahead = pack(own(e2 | e3, row, rows) + take(first, order.index(7)))
        behind = pack(own(e2, row, rows) + take(first, order.index(e1 | e2)))
        seconds.append((exchange(ahead, e2), exchange(behind, e2)))
    packed = [
        pack(own(e3, row, rows) + take(first, order.index(e1 | e3)) + ahead.astype(jnp.float32))
        for (row, rows, (e1, e2, e3)), (first, order), (ahead, _) in zip(PARTS, firsts, seconds)
    ]
    thirds = [exchange(message, e3) for message, (_, _, (_, _, e3)) in zip(packed, PARTS)]
    acc_near, _ = lax.optimization_barrier((acc_near, packed))
    pieces = [
        own(0, row, rows)
        + last.astype(jnp.float32)
        + behind.astype(jnp.float32)
        + third.astype(jnp.float32)
        for (row, rows, _), last, (_, behind), third in zip(PARTS, lasts, seconds, thirds)
    ]

    all_squares = lax.all_to_all(squares_of(pieces), "fsdp", 0, 0, tiled=True)
    updated, clip = adam(step_index, all_squares, pieces, weights, first_moment, second_moment)
    outs = lax.switch(
        step_bit,
        [partial(finish, apart) for apart in range(4)],
        pack(updated),
        updated,
        clip,
        pieces,
        first_moment,
        second_moment,
    )
    return tuple(out[None] for out in outs)


def solution(mesh):
    spec = P("replica", "fsdp", None)
    return jax.shard_map(
        local,
        mesh=mesh,
        in_specs=(spec, spec, spec, spec, spec, P()),
        out_specs=(spec, spec, spec),
        check_vma=False,
    )
```

```python
from functools import partial
import math

import jax
import jax.numpy as jnp
from jax import lax
from jax.experimental import pallas as pl
from jax.experimental.pallas import tpu as pltpu
from jax.sharding import PartitionSpec as P

BETA_ONE = 0.9
BETA_TWO = 0.95
LEARN_RATE = 0.08
ADAM_EPS = 1e-08
NORM_EPS = 1e-06

SEND_SCALE = 2.0**-8
RAISE = 2.0**8

X, A, B = 1, 2, 4
PARTS = ((0, 176, (X, A, B)), (176, 176, (A, B, X)), (352, 160, (B, X, A)))


def neighbour(i, dim):
    y, x, c = i >> 2, (i >> 1) & 1, i & 1
    g = y ^ (y >> 1)
    if dim == X:
        x ^= 1
    elif dim == A:
        g ^= 1
    elif dim == B:
        g ^= 2
    else:
        c ^= 1
    y = g ^ (g >> 1)
    return (y << 2) | (x << 1) | c


def exchange(array, dim):
    return lax.ppermute(array, "fsdp", [(i, neighbour(i, dim)) for i in range(16)])


def from_partner(apart, array):
    return lax.ppermute(array, "replica", [(i, i ^ 1 << apart) for i in range(16)])


def block_of(me, d, flip):
    y, x, c = me >> 2, (me >> 1) & 1, me & 1
    g = (y ^ (y >> 1)) ^ (d >> 1)
    return ((g ^ (g >> 1)) << 2) | ((x ^ (d & 1)) << 1) | (c ^ flip)


FAR = (7, 5, 3, 6)
NEAR = (1, 2, 4, 0)
PAIR = {X: (slice(1, 3), (5, 3)), A: (slice(2, 4), (3, 6)), B: (slice(1, 4, 2), (5, 6))}
VMEM_LIMIT = 24 << 20


def fetch_kernel(wanted, me, tokens, grads, *refs):
    *outs, sems = refs
    copies = []
    for out, (order, flip, _) in zip(outs, wanted):
        for j in range(4):
            column = pl.multiple_of(block_of(me[0], order[j], flip) * 512, 512)
            copies.append(
                pltpu.make_async_copy(
                    tokens.at[:, pl.ds(column, 512)],
                    out.at[:, pl.ds(j * 512, 512)],
                    sems.at[len(copies)],
                )
            )
        if out.shape[1] > 2048:
            copies.append(
                pltpu.make_async_copy(grads, out.at[:, pl.ds(2048, 512)], sems.at[len(copies)])
            )
    for copy in copies:
        copy.start()
    for copy in copies:
        copy.wait()


def fetch(me, tokens, grads, wanted):
    t = tokens.shape[0]
    return pl.pallas_call(
        partial(fetch_kernel, wanted),
        in_specs=[
            pl.BlockSpec(memory_space=pltpu.SMEM),
            pl.BlockSpec(memory_space=pltpu.HBM),
            pl.BlockSpec(memory_space=pltpu.HBM),
        ],
        out_shape=[pltpu.VMEM((t, width), tokens.dtype) for _, _, width in wanted],
        scratch_shapes=[pltpu.SemaphoreType.DMA((5 * len(wanted),))],
        cost_estimate=pl.CostEstimate(
            flops=0, bytes_accessed=4 * t * 2048 * len(wanted), transcendentals=0
        ),
        compiler_params=pltpu.CompilerParams(vmem_limit_bytes=VMEM_LIMIT),
        name="fetch",
    )(
        me,
        pltpu.with_memory_space_constraint(tokens, pltpu.HBM),
        pltpu.with_memory_space_constraint(grads, pltpu.HBM),
    )


def hold_kernel(*refs):
    *pairs, sems = refs
    n = len(pairs) // 2
    copies = [pltpu.make_async_copy(pairs[i], pairs[n + i], sems.at[i]) for i in range(n)]
    for copy in copies:
        copy.start()
    for copy in copies:
        copy.wait()


def hold(*arrays):
    return pl.pallas_call(
        hold_kernel,
        in_specs=[pl.BlockSpec(memory_space=pltpu.HBM)] * len(arrays),
        out_shape=[pltpu.VMEM(a.shape, a.dtype) for a in arrays],
        scratch_shapes=[pltpu.SemaphoreType.DMA((len(arrays),))],
        compiler_params=pltpu.CompilerParams(vmem_limit_bytes=VMEM_LIMIT),
        name="hold",
    )(*[pltpu.with_memory_space_constraint(a, pltpu.HBM) for a in arrays])


def product_kernel(mine, theirs, g_mine, g_theirs, out, tokens, grads):
    t = g_mine.shape[0]
    grads[:t] = g_mine[:, 2048:]
    grads[t:] = g_theirs[:, 2048:]

    def block(j, _):
        column = pl.multiple_of(j * 512, 512)
        tokens[:t] = mine[:, pl.ds(column, 512)]
        tokens[t:] = theirs[:, pl.ds(column, 512)]
        out[j] = lax.dot_general(
            tokens[...], grads[...], (((0,), (0,)), ((), ())), preferred_element_type=jnp.float32
        )
        return _

    lax.fori_loop(0, 4, block, None)


def product(mine, theirs, g_mine, g_theirs):
    t, k = g_mine.shape[0], 512
    vmem = pl.BlockSpec(memory_space=pltpu.VMEM)
    return pl.pallas_call(
        product_kernel,
        in_specs=[vmem] * 4,
        out_specs=vmem,
        scratch_shapes=[pltpu.VMEM((2 * t, 512), mine.dtype), pltpu.VMEM((2 * t, k), mine.dtype)],
        out_shape=jax.ShapeDtypeStruct((4, 512, k), jnp.float32),
        cost_estimate=pl.CostEstimate(
            flops=2 * 2 * t * 2048 * k, bytes_accessed=4 * t * 2048 + 16 * 512 * k, transcendentals=0
        ),
        compiler_params=pltpu.CompilerParams(vmem_limit_bytes=VMEM_LIMIT),
        name="product",
    )(mine, theirs, g_mine, g_theirs)


def squares_kernel(*refs):
    *pieces, out = refs
    total = sum(jnp.sum((p[...] * p[...]).reshape(-1, 8, 512), axis=0) for p in pieces)
    total = total[:, :128] + total[:, 128:256] + total[:, 256:384] + total[:, 384:]
    total = jnp.sum(total, axis=0, keepdims=True)
    out[...] = jnp.broadcast_to(total[None], out.shape)


def squares_of(pieces):
    return pl.pallas_call(
        squares_kernel,
        out_shape=jax.ShapeDtypeStruct((16, 1, 128), jnp.float32),
        compiler_params=pltpu.CompilerParams(vmem_limit_bytes=VMEM_LIMIT),
        name="squares",
    )(*pieces)


def adam_kernel(step_index, all_squares, *refs):
    *pieces, weights, first, second, updated, clip_out = refs
    squares = jnp.sum(all_squares[...], axis=0)
    squares = jnp.sum(squares, axis=1, keepdims=True)
    norm = jnp.sqrt(squares) * RAISE
    clip = jnp.minimum(1.0, math.sqrt(8192 * 512) / (norm + NORM_EPS)) * RAISE
    clip_out[...] = jnp.broadcast_to(clip, clip_out.shape)
    steps = jnp.full((1, 1), step_index[0] + 1, jnp.int32).astype(jnp.float32)
    rate = LEARN_RATE / (1.0 - jnp.exp(steps * math.log(BETA_ONE)))
    second_scale = 1.0 / (1.0 - jnp.exp(steps * math.log(BETA_TWO)))
    row = 0
    for piece in pieces:
        rows = pl.ds(row, piece.shape[0])
        row += piece.shape[0]
        clipped = clip * piece[...]
        one = BETA_ONE * first[rows] + (1.0 - BETA_ONE) * clipped
        two = BETA_TWO * second[rows] + (1.0 - BETA_TWO) * clipped * clipped
        updated[rows] = weights[rows] - rate * one / (jnp.sqrt(two * second_scale) + ADAM_EPS)


def adam(step_index, all_squares, pieces, weights, first, second):
    vmem = pl.BlockSpec(memory_space=pltpu.VMEM)
    return pl.pallas_call(
        adam_kernel,
        in_specs=[pl.BlockSpec(memory_space=pltpu.SMEM)] + [vmem] * (len(pieces) + 4),
        out_specs=[vmem] * 2,
        out_shape=[
            jax.ShapeDtypeStruct(weights.shape, jnp.float32),
            jax.ShapeDtypeStruct((8, 512), jnp.float32),
        ],
        compiler_params=pltpu.CompilerParams(vmem_limit_bytes=VMEM_LIMIT),
        name="adam",
    )(step_index, all_squares, *pieces, weights, first, second)


def moments_kernel(clip, *refs):
    *pieces, first, second, new_first, new_second = refs
    row = 0
    for piece in pieces:
        rows = pl.ds(row, piece.shape[0])
        row += piece.shape[0]
        clipped = clip[:1] * piece[...]
        new_first[rows] = BETA_ONE * first[rows] + (1.0 - BETA_ONE) * clipped
        new_second[rows] = BETA_TWO * second[rows] + (1.0 - BETA_TWO) * clipped * clipped


def moments(clip, pieces, first, second):
    vmem = pl.BlockSpec(memory_space=pltpu.VMEM)
    return pl.pallas_call(
        moments_kernel,
        in_specs=[vmem] * (len(pieces) + 3),
        out_specs=[vmem] * 2,
        out_shape=[jax.ShapeDtypeStruct(first.shape, jnp.float32)] * 2,
        cost_estimate=pl.CostEstimate(
            flops=8 * first.size, bytes_accessed=20 * first.size, transcendentals=0
        ),
        compiler_params=pltpu.CompilerParams(vmem_limit_bytes=VMEM_LIMIT),
        name="moments",
    )(clip, *pieces, first, second)


def finish(apart, packed, updated, clip, pieces, first, second):
    theirs = from_partner(apart, packed)
    new_first, new_second = moments(clip, pieces, first, second)
    new_weights = 0.5 * (updated + theirs.astype(jnp.float32))
    return new_weights, new_first, new_second


def local(tokens, key_grads, weights, first_moment, second_moment, step_index):
    inputs = tokens[0]
    grads_out = key_grads[0]
    step_bit = step_index[0] % 4
    me, step_bit = lax.optimization_barrier((lax.axis_index("fsdp")[None], step_bit))

    far_out, mine_far = fetch(me, inputs, grads_out, ((FAR, 1, 2560), (FAR, 0, 2560)))
    theirs_far = exchange(far_out, 0)
    near_out, mine_near = fetch(me, inputs, grads_out, ((NEAR, 1, 2048), (NEAR, 0, 2048)))
    theirs_near = exchange(near_out, 0)
    acc_far = product(mine_far, theirs_far, mine_far, theirs_far)
    acc_near = product(mine_near, theirs_near, mine_far, theirs_far)

    def own(d, row, rows):
        source, slot = (acc_far, FAR.index(d)) if d in FAR else (acc_near, NEAR.index(d))
        return source[slot, row : row + rows] * SEND_SCALE

    def pack(array):
        return array.astype(jnp.float16)

    parts = {dim: [p for at in range(3) for p in PARTS if p[2][at] == dim] for dim in (X, A, B)}
    packed = {}
    for dim in (X, A, B):
        row, rows, _ = parts[dim][0]
        packed[dim] = pack(own(7, row, rows))
    corner = {dim: exchange(packed[dim], dim) for dim in packed}
    for dim in (X, A, B):
        row, rows, _ = parts[dim][0]
        packed[dim] = pack(acc_far[PAIR[dim][0], row : row + rows] * SEND_SCALE)
    pairs = {dim: exchange(packed[dim], dim) for dim in packed}

    def from_pair(dim, d):
        return pairs[dim][PAIR[dim][1].index(d)].astype(jnp.float32)

    for dim in (X, A, B):
        row, rows, (e1, e2, e3) = parts[dim][1]
        packed[dim] = pack(own(e2 | e3, row, rows) + corner[e1].astype(jnp.float32))
    ahead = {dim: exchange(packed[dim], dim) for dim in packed}
    acc_near, weights, first_moment, second_moment, _ = lax.optimization_barrier(
        (acc_near, weights[0], first_moment[0], second_moment[0], packed)
    )
    weights, first_moment, second_moment = hold(weights, first_moment, second_moment)
    acc_near, weights, first_moment, second_moment = lax.optimization_barrier(
        (acc_near, weights, first_moment, second_moment)
    )
    for dim in (X, A, B):
        row, rows, _ = parts[dim][0]
        last = own(dim, row, rows)
        row, rows, (e1, e2, e3) = parts[dim][1]
        behind = own(e2, row, rows) + from_pair(e1, e1 | e2)
        packed[dim] = pack(jnp.concatenate([last, behind]))
    rests = {dim: exchange(packed[dim], dim) for dim in packed}
    acc_near, _ = lax.optimization_barrier((acc_near, packed))
    for dim in (X, A, B):
        row, rows, (e1, e2, e3) = parts[dim][2]
        packed[dim] = pack(
            own(e3, row, rows) + from_pair(e1, e1 | e3) + ahead[e2].astype(jnp.float32)
        )
    thirds = {dim: exchange(packed[dim], dim) for dim in packed}
    acc_near, _ = lax.optimization_barrier((acc_near, packed))
    pieces = [
        own(0, row, rows)
        + rests[e1][:rows].astype(jnp.float32)
        + rests[e2][-rows:].astype(jnp.float32)
        + thirds[e3].astype(jnp.float32)
        for row, rows, (e1, e2, e3) in PARTS
    ]

    all_squares = lax.all_to_all(squares_of(pieces), "fsdp", 0, 0, tiled=True)
    updated, clip = adam(step_index, all_squares, pieces, weights, first_moment, second_moment)
    outs = lax.switch(
        step_bit,
        [partial(finish, apart) for apart in range(4)],
        pack(updated),
        updated,
        clip,
        pieces,
        first_moment,
        second_moment,
    )
    return tuple(out[None] for out in outs)


def solution(mesh):
    spec = P("replica", "fsdp", None)
    return jax.shard_map(
        local,
        mesh=mesh,
        in_specs=(spec, spec, spec, spec, spec, P()),
        out_specs=(spec, spec, spec),
        check_vma=False,
    )
```

```python
from functools import partial
import math

import jax
import jax.numpy as jnp
from jax import lax
from jax._src.lax.control_flow import conditionals
from jax.experimental import pallas as pl
from jax.experimental.pallas import tpu as pltpu
from jax.sharding import PartitionSpec as P

BETA_ONE = 0.9
BETA_TWO = 0.95
LEARN_RATE = 0.08
ADAM_EPS = 1e-08
NORM_EPS = 1e-06

SEND_SCALE = 2.0**-8
RAISE = 2.0**8

X, A, B = 1, 2, 4
PARTS = ((0, 176, (X, A, B)), (176, 176, (A, B, X)), (352, 160, (B, X, A)))


def neighbour(i, dim):
    y, x, c = i >> 2, (i >> 1) & 1, i & 1
    g = y ^ (y >> 1)
    if dim == X:
        x ^= 1
    elif dim == A:
        g ^= 1
    elif dim == B:
        g ^= 2
    else:
        c ^= 1
    y = g ^ (g >> 1)
    return (y << 2) | (x << 1) | c


def exchange(array, dim):
    return lax.ppermute(array, "fsdp", [(i, neighbour(i, dim)) for i in range(16)])


def from_partner(apart, array):
    return lax.ppermute(array, "replica", [(i, i ^ 1 << apart) for i in range(16)])


def block_of(me, d, flip):
    y, x, c = me >> 2, (me >> 1) & 1, me & 1
    g = (y ^ (y >> 1)) ^ (d >> 1)
    return ((g ^ (g >> 1)) << 2) | ((x ^ (d & 1)) << 1) | (c ^ flip)


FAR = (7, 5, 3, 6)
NEAR = (1, 2, 4, 0)
PAIR = {X: (slice(1, 3), (5, 3)), A: (slice(2, 4), (3, 6)), B: (slice(1, 4, 2), (5, 6))}
VMEM_LIMIT = 24 << 20


def fetch_kernel(wanted, me, step_index, tokens, grads, *refs):
    *outs, level, sems = refs
    level[0] = step_index[0] % 4
    copies = []
    for out, (order, flip, _) in zip(outs, wanted):
        for j in range(4):
            column = pl.multiple_of(block_of(me[0], order[j], flip) * 512, 512)
            copies.append(
                pltpu.make_async_copy(
                    tokens.at[:, pl.ds(column, 512)],
                    out.at[:, pl.ds(j * 512, 512)],
                    sems.at[len(copies)],
                )
            )
        if out.shape[1] > 2048:
            copies.append(
                pltpu.make_async_copy(grads, out.at[:, pl.ds(2048, 512)], sems.at[len(copies)])
            )
    for copy in copies:
        copy.start()
    for copy in copies:
        copy.wait()


def fetch(me, step_index, tokens, grads, wanted):
    t = tokens.shape[0]
    return pl.pallas_call(
        partial(fetch_kernel, wanted),
        in_specs=[
            pl.BlockSpec(memory_space=pltpu.SMEM),
            pl.BlockSpec(memory_space=pltpu.SMEM),
            pl.BlockSpec(memory_space=pltpu.HBM),
            pl.BlockSpec(memory_space=pltpu.HBM),
        ],
        out_specs=[pl.BlockSpec(memory_space=pltpu.VMEM)] * len(wanted)
        + [pl.BlockSpec(memory_space=pltpu.SMEM)],
        out_shape=[pltpu.VMEM((t, width), tokens.dtype) for _, _, width in wanted]
        + [jax.ShapeDtypeStruct((1,), jnp.int32)],
        scratch_shapes=[pltpu.SemaphoreType.DMA((5 * len(wanted),))],
        cost_estimate=pl.CostEstimate(
            flops=0, bytes_accessed=4 * t * 2048 * len(wanted), transcendentals=0
        ),
        compiler_params=pltpu.CompilerParams(vmem_limit_bytes=VMEM_LIMIT),
        name="fetch",
    )(
        me,
        step_index,
        pltpu.with_memory_space_constraint(tokens, pltpu.HBM),
        pltpu.with_memory_space_constraint(grads, pltpu.HBM),
    )


def hold_kernel(*refs):
    *pairs, sems = refs
    n = len(pairs) // 2
    copies = [pltpu.make_async_copy(pairs[i], pairs[n + i], sems.at[i]) for i in range(n)]
    for copy in copies:
        copy.start()
    for copy in copies:
        copy.wait()


def hold(*arrays):
    return pl.pallas_call(
        hold_kernel,
        in_specs=[pl.BlockSpec(memory_space=pltpu.HBM)] * len(arrays),
        out_shape=[pltpu.VMEM(a.shape, a.dtype) for a in arrays],
        scratch_shapes=[pltpu.SemaphoreType.DMA((len(arrays),))],
        compiler_params=pltpu.CompilerParams(vmem_limit_bytes=VMEM_LIMIT),
        name="hold",
    )(*[pltpu.with_memory_space_constraint(a, pltpu.HBM) for a in arrays])


def product_kernel(mine, theirs, g_mine, g_theirs, out, tokens, grads):
    t = g_mine.shape[0]
    grads[:t] = g_mine[:, 2048:]
    grads[t:] = g_theirs[:, 2048:]

    def block(j, _):
        column = pl.multiple_of(j * 512, 512)
        tokens[:t] = mine[:, pl.ds(column, 512)]
        tokens[t:] = theirs[:, pl.ds(column, 512)]
        out[j] = lax.dot_general(
            tokens[...], grads[...], (((0,), (0,)), ((), ())), preferred_element_type=jnp.float32
        )
        return _

    lax.fori_loop(0, 4, block, None)


def product(mine, theirs, g_mine, g_theirs):
    t, k = g_mine.shape[0], 512
    vmem = pl.BlockSpec(memory_space=pltpu.VMEM)
    return pl.pallas_call(
        product_kernel,
        in_specs=[vmem] * 4,
        out_specs=vmem,
        scratch_shapes=[pltpu.VMEM((2 * t, 512), mine.dtype), pltpu.VMEM((2 * t, k), mine.dtype)],
        out_shape=jax.ShapeDtypeStruct((4, 512, k), jnp.float32),
        cost_estimate=pl.CostEstimate(
            flops=2 * 2 * t * 2048 * k, bytes_accessed=4 * t * 2048 + 16 * 512 * k, transcendentals=0
        ),
        compiler_params=pltpu.CompilerParams(vmem_limit_bytes=VMEM_LIMIT),
        name="product",
    )(mine, theirs, g_mine, g_theirs)


def squares_kernel(*refs):
    *pieces, out = refs
    total = sum(jnp.sum((p[...] * p[...]).reshape(-1, 8, 512), axis=0) for p in pieces)
    total = total[:, :128] + total[:, 128:256] + total[:, 256:384] + total[:, 384:]
    total = jnp.sum(total, axis=0, keepdims=True)
    out[...] = jnp.broadcast_to(total[None], out.shape)


def squares_of(pieces):
    return pl.pallas_call(
        squares_kernel,
        out_shape=jax.ShapeDtypeStruct((16, 1, 128), jnp.float32),
        compiler_params=pltpu.CompilerParams(vmem_limit_bytes=VMEM_LIMIT),
        name="squares",
    )(*pieces)


def adam_kernel(step_index, all_squares, *refs):
    *pieces, weights, first, second, updated, clip_out = refs
    squares = jnp.sum(all_squares[...], axis=0)
    squares = jnp.sum(squares, axis=1, keepdims=True)
    norm = jnp.sqrt(squares) * RAISE
    clip = jnp.minimum(1.0, math.sqrt(8192 * 512) / (norm + NORM_EPS)) * RAISE
    clip_out[...] = jnp.broadcast_to(clip, clip_out.shape)
    steps = jnp.full((1, 1), step_index[0] + 1, jnp.int32).astype(jnp.float32)
    rate = LEARN_RATE / (1.0 - jnp.exp(steps * math.log(BETA_ONE)))
    second_scale = 1.0 / (1.0 - jnp.exp(steps * math.log(BETA_TWO)))
    row = 0
    for piece in pieces:
        rows = pl.ds(row, piece.shape[0])
        row += piece.shape[0]
        clipped = clip * piece[...]
        one = BETA_ONE * first[rows] + (1.0 - BETA_ONE) * clipped
        two = BETA_TWO * second[rows] + (1.0 - BETA_TWO) * clipped * clipped
        updated[rows] = weights[rows] - rate * one / (jnp.sqrt(two * second_scale) + ADAM_EPS)


def adam(step_index, all_squares, pieces, weights, first, second):
    vmem = pl.BlockSpec(memory_space=pltpu.VMEM)
    return pl.pallas_call(
        adam_kernel,
        in_specs=[pl.BlockSpec(memory_space=pltpu.SMEM)] + [vmem] * (len(pieces) + 4),
        out_specs=[vmem] * 2,
        out_shape=[
            jax.ShapeDtypeStruct(weights.shape, jnp.float32),
            jax.ShapeDtypeStruct((8, 512), jnp.float32),
        ],
        compiler_params=pltpu.CompilerParams(vmem_limit_bytes=VMEM_LIMIT),
        name="adam",
    )(step_index, all_squares, *pieces, weights, first, second)


def moments_kernel(clip, *refs):
    *pieces, first, second, new_first, new_second = refs
    row = 0
    for piece in pieces:
        rows = pl.ds(row, piece.shape[0])
        row += piece.shape[0]
        clipped = clip[:1] * piece[...]
        new_first[rows] = BETA_ONE * first[rows] + (1.0 - BETA_ONE) * clipped
        new_second[rows] = BETA_TWO * second[rows] + (1.0 - BETA_TWO) * clipped * clipped


def moments(clip, pieces, first, second):
    vmem = pl.BlockSpec(memory_space=pltpu.VMEM)
    return pl.pallas_call(
        moments_kernel,
        in_specs=[vmem] * (len(pieces) + 3),
        out_specs=[vmem] * 2,
        out_shape=[jax.ShapeDtypeStruct(first.shape, jnp.float32)] * 2,
        cost_estimate=pl.CostEstimate(
            flops=8 * first.size, bytes_accessed=20 * first.size, transcendentals=0
        ),
        compiler_params=pltpu.CompilerParams(vmem_limit_bytes=VMEM_LIMIT),
        name="moments",
    )(clip, *pieces, first, second)


def finish(apart, packed, updated, clip, pieces, first, second):
    theirs = from_partner(apart, packed)
    new_first, new_second = moments(clip, pieces, first, second)
    new_weights = 0.5 * (updated + theirs.astype(jnp.float32))
    return new_weights, new_first, new_second


def local(tokens, key_grads, weights, first_moment, second_moment, step_index):
    inputs = tokens[0]
    grads_out = key_grads[0]
    me = lax.axis_index("fsdp")[None]

    far_out, _ = fetch(me, me, inputs, grads_out, ((FAR, 1, 2560),))
    theirs_far = exchange(far_out, 0)
    mine_far, near_out, mine_near, level = fetch(
        me, step_index, inputs, grads_out, ((FAR, 0, 2560), (NEAR, 1, 2048), (NEAR, 0, 2048))
    )
    theirs_near = exchange(near_out, 0)
    acc_far = product(mine_far, theirs_far, mine_far, theirs_far)
    acc_near = product(mine_near, theirs_near, mine_far, theirs_far)

    def own(d, row, rows):
        source, slot = (acc_far, FAR.index(d)) if d in FAR else (acc_near, NEAR.index(d))
        return source[slot, row : row + rows] * SEND_SCALE

    def pack(array):
        return array.astype(jnp.float16)

    parts = {dim: [p for at in range(3) for p in PARTS if p[2][at] == dim] for dim in (X, A, B)}
    packed = {}
    for dim in (X, A, B):
        row, rows, _ = parts[dim][0]
        packed[dim] = pack(own(7, row, rows))
    corner = {dim: exchange(packed[dim], dim) for dim in packed}
    for dim in (X, A, B):
        row, rows, _ = parts[dim][0]
        packed[dim] = pack(acc_far[PAIR[dim][0], row : row + rows] * SEND_SCALE)
    pairs = {dim: exchange(packed[dim], dim) for dim in packed}

    def from_pair(dim, d):
        return pairs[dim][PAIR[dim][1].index(d)].astype(jnp.float32)

    for dim in (X, A, B):
        row, rows, (e1, e2, e3) = parts[dim][1]
        packed[dim] = pack(own(e2 | e3, row, rows) + corner[e1].astype(jnp.float32))
    ahead = {dim: exchange(packed[dim], dim) for dim in packed}
    acc_near, weights, first_moment, second_moment, _ = lax.optimization_barrier(
        (acc_near, weights[0], first_moment[0], second_moment[0], packed)
    )
    weights, first_moment, second_moment = hold(weights, first_moment, second_moment)
    acc_near, weights, first_moment, second_moment = lax.optimization_barrier(
        (acc_near, weights, first_moment, second_moment)
    )
    for dim in (X, A, B):
        row, rows, _ = parts[dim][0]
        last = own(dim, row, rows)
        row, rows, (e1, e2, e3) = parts[dim][1]
        behind = own(e2, row, rows) + from_pair(e1, e1 | e2)
        packed[dim] = pack(jnp.concatenate([last, behind]))
    rests = {dim: exchange(packed[dim], dim) for dim in packed}
    acc_near, _ = lax.optimization_barrier((acc_near, packed))
    for dim in (X, A, B):
        row, rows, (e1, e2, e3) = parts[dim][2]
        packed[dim] = pack(
            own(e3, row, rows) + from_pair(e1, e1 | e3) + ahead[e2].astype(jnp.float32)
        )
    thirds = {dim: exchange(packed[dim], dim) for dim in packed}
    acc_near, _ = lax.optimization_barrier((acc_near, packed))
    pieces = [
        own(0, row, rows)
        + rests[e1][:rows].astype(jnp.float32)
        + rests[e2][-rows:].astype(jnp.float32)
        + thirds[e3].astype(jnp.float32)
        for row, rows, (e1, e2, e3) in PARTS
    ]

    all_squares = lax.all_to_all(squares_of(pieces), "fsdp", 0, 0, tiled=True)
    updated, clip = adam(step_index, all_squares, pieces, weights, first_moment, second_moment)
    outs = conditionals._switch_internal(
        level[0],
        [partial(finish, apart) for apart in range(4)],
        (pack(updated), updated, clip, pieces, first_moment, second_moment),
        branches_platforms=None,
    )
    return tuple(out[None] for out in outs)


def solution(mesh):
    spec = P("replica", "fsdp", None)
    return jax.shard_map(
        local,
        mesh=mesh,
        in_specs=(spec, spec, spec, spec, spec, P()),
        out_specs=(spec, spec, spec),
        check_vma=False,
    )
```

```python
from functools import partial
import math

import jax
import jax.numpy as jnp
from jax import lax
from jax._src.lax.control_flow import conditionals
from jax.experimental import pallas as pl
from jax.experimental.pallas import tpu as pltpu
from jax.sharding import PartitionSpec as P


BETA_ONE = 0.9
BETA_TWO = 0.95
LEARN_RATE = 0.08
ADAM_EPS = 1e-08
NORM_EPS = 1e-06

SEND_SCALE = 2.0**-8
RAISE = 2.0**8

X, A, B = 1, 2, 4
PARTS = ((0, 176, (X, A, B)), (176, 176, (A, B, X)), (352, 160, (B, X, A)))


def neighbour(i, dim):
    y, x, c = i >> 2, (i >> 1) & 1, i & 1
    g = y ^ (y >> 1)
    if dim == X:
        x ^= 1
    elif dim == A:
        g ^= 1
    elif dim == B:
        g ^= 2
    else:
        c ^= 1
    y = g ^ (g >> 1)
    return (y << 2) | (x << 1) | c


def exchange(array, dim):
    return lax.ppermute(array, "fsdp", [(i, neighbour(i, dim)) for i in range(16)])


def from_partner(apart, array):
    return lax.ppermute(array, "replica", [(i, i ^ 1 << apart) for i in range(16)])


def block_of(me, d, flip):
    y, x, c = me >> 2, (me >> 1) & 1, me & 1
    g = (y ^ (y >> 1)) ^ (d >> 1)
    return ((g ^ (g >> 1)) << 2) | ((x ^ (d & 1)) << 1) | (c ^ flip)


CORNER = (7,)
FAR = (5, 3, 6)
NEAR = (1, 2, 4, 0)
PAIR = {X: (slice(0, 2), (5, 3)), A: (slice(1, 3), (3, 6)), B: (slice(0, 3, 2), (5, 6))}
VMEM_LIMIT = 24 << 20


def start_fetch(wanted, me, tokens, grads, outs, sems):
    copies = []
    for out, (order, flip) in zip(outs, wanted):
        for j, d in enumerate(order):
            column = pl.multiple_of(block_of(me[0], d, flip) * 512, 512)
            copies.append(
                pltpu.make_async_copy(
                    tokens.at[:, pl.ds(column, 512)],
                    out.at[:, pl.ds(j * 512, 512)],
                    sems.at[len(copies)],
                )
            )
        if out.shape[1] > 512 * len(order):
            copies.append(
                pltpu.make_async_copy(
                    grads, out.at[:, pl.ds(512 * len(order), 512)], sems.at[len(copies)]
                )
            )
    for copy in copies:
        copy.start()
    return copies


def fetch_kernel(wanted, me, tokens, grads, *refs):
    *outs, sems = refs
    for copy in start_fetch(wanted, me, tokens, grads, outs, sems):
        copy.wait()


def fetch(me, tokens, grads, wanted, widths):
    t = tokens.shape[0]
    return pl.pallas_call(
        partial(fetch_kernel, wanted),
        in_specs=[
            pl.BlockSpec(memory_space=pltpu.SMEM),
            pl.BlockSpec(memory_space=pltpu.HBM),
            pl.BlockSpec(memory_space=pltpu.HBM),
        ],
        out_shape=[pltpu.VMEM((t, width), tokens.dtype) for width in widths],
        scratch_shapes=[pltpu.SemaphoreType.DMA((8,))],
        cost_estimate=pl.CostEstimate(
            flops=0, bytes_accessed=4 * t * sum(widths), transcendentals=0
        ),
        compiler_params=pltpu.CompilerParams(vmem_limit_bytes=VMEM_LIMIT),
        name="fetch",
    )(
        me,
        pltpu.with_memory_space_constraint(tokens, pltpu.HBM),
        pltpu.with_memory_space_constraint(grads, pltpu.HBM),
    )


def hold_kernel(*refs):
    *pairs, sems = refs
    n = len(pairs) // 2
    copies = [pltpu.make_async_copy(pairs[i], pairs[n + i], sems.at[i]) for i in range(n)]
    for copy in copies:
        copy.start()
    for copy in copies:
        copy.wait()


def hold(*arrays):
    return pl.pallas_call(
        hold_kernel,
        in_specs=[pl.BlockSpec(memory_space=pltpu.HBM)] * len(arrays),
        out_shape=[pltpu.VMEM(a.shape, a.dtype) for a in arrays],
        scratch_shapes=[pltpu.SemaphoreType.DMA((len(arrays),))],
        compiler_params=pltpu.CompilerParams(vmem_limit_bytes=VMEM_LIMIT),
        name="hold",
    )(*[pltpu.with_memory_space_constraint(a, pltpu.HBM) for a in arrays])


def product_kernel(wanted, me, step_index, tokens, grads, mine, theirs, g_mine, g_theirs, *refs):
    out, level, *outs, both_tokens, both_grads, sems = refs
    t = g_mine.shape[0]
    copies = start_fetch(wanted, me, tokens, grads, outs, sems)
    level[0] = step_index[0] % 4
    both_grads[:t] = g_mine[:, 512:]
    both_grads[t:] = g_theirs[:, 512:]

    def block(j, _):
        column = pl.multiple_of(j * 512, 512)
        both_tokens[:t] = mine[:, pl.ds(column, 512)]
        both_tokens[t:] = theirs[:, pl.ds(column, 512)]
        out[j] = lax.dot_general(
            both_tokens[...],
            both_grads[...],
            (((0,), (0,)), ((), ())),
            preferred_element_type=jnp.float32,
        )
        return _

    lax.fori_loop(0, out.shape[0], block, None)
    for copy in copies:
        copy.wait()


def product(me, step_index, tokens, grads, mine, theirs, g_mine, g_theirs, blocks, wanted, widths):
    t, k = g_mine.shape[0], 512
    vmem = pl.BlockSpec(memory_space=pltpu.VMEM)
    smem = pl.BlockSpec(memory_space=pltpu.SMEM)
    hbm = pl.BlockSpec(memory_space=pltpu.HBM)
    return pl.pallas_call(
        partial(product_kernel, wanted),
        in_specs=[smem, smem, hbm, hbm] + [vmem] * 4,
        out_specs=[vmem, smem] + [vmem] * len(wanted),
        scratch_shapes=[
            pltpu.VMEM((2 * t, 512), mine.dtype),
            pltpu.VMEM((2 * t, k), mine.dtype),
            pltpu.SemaphoreType.DMA((8,)),
        ],
        out_shape=[
            pltpu.VMEM((blocks, 512, k), jnp.float32),
            jax.ShapeDtypeStruct((1,), jnp.int32),
        ]
        + [pltpu.VMEM((t, width), tokens.dtype) for width in widths],
        cost_estimate=pl.CostEstimate(
            flops=4 * t * 512 * blocks * k, bytes_accessed=4 * t * sum(widths), transcendentals=0
        ),
        compiler_params=pltpu.CompilerParams(vmem_limit_bytes=VMEM_LIMIT),
        name="product",
    )(
        me,
        step_index,
        pltpu.with_memory_space_constraint(tokens, pltpu.HBM),
        pltpu.with_memory_space_constraint(grads, pltpu.HBM),
        mine,
        theirs,
        g_mine,
        g_theirs,
    )


def squares_kernel(*refs):
    *pieces, out = refs
    total = sum(jnp.sum((p[...] * p[...]).reshape(-1, 8, 512), axis=0) for p in pieces)
    total = total[:, :128] + total[:, 128:256] + total[:, 256:384] + total[:, 384:]
    total = jnp.sum(total, axis=0, keepdims=True)
    out[...] = jnp.broadcast_to(total[None], out.shape)


def squares_of(pieces):
    return pl.pallas_call(
        squares_kernel,
        out_shape=jax.ShapeDtypeStruct((16, 1, 128), jnp.float32),
        compiler_params=pltpu.CompilerParams(vmem_limit_bytes=VMEM_LIMIT),
        name="squares",
    )(*pieces)


def adam_kernel(step_index, all_squares, *refs):
    *pieces, weights, first, second, updated, clip_out = refs
    squares = jnp.sum(all_squares[...], axis=0)
    squares = jnp.sum(squares, axis=1, keepdims=True)
    norm = jnp.sqrt(squares) * RAISE
    clip = jnp.minimum(1.0, math.sqrt(8192 * 512) / (norm + NORM_EPS)) * RAISE
    clip_out[...] = jnp.broadcast_to(clip, clip_out.shape)
    steps = jnp.full((1, 1), step_index[0] + 1, jnp.int32).astype(jnp.float32)
    rate = LEARN_RATE / (1.0 - jnp.exp(steps * math.log(BETA_ONE)))
    second_scale = 1.0 / (1.0 - jnp.exp(steps * math.log(BETA_TWO)))
    row = 0
    for piece in pieces:
        rows = pl.ds(row, piece.shape[0])
        row += piece.shape[0]
        clipped = clip * piece[...]
        one = BETA_ONE * first[rows] + (1.0 - BETA_ONE) * clipped
        two = BETA_TWO * second[rows] + (1.0 - BETA_TWO) * clipped * clipped
        updated[rows] = weights[rows] - rate * one / (jnp.sqrt(two * second_scale) + ADAM_EPS)


def adam(step_index, all_squares, pieces, weights, first, second):
    vmem = pl.BlockSpec(memory_space=pltpu.VMEM)
    return pl.pallas_call(
        adam_kernel,
        in_specs=[pl.BlockSpec(memory_space=pltpu.SMEM)] + [vmem] * (len(pieces) + 4),
        out_specs=[vmem] * 2,
        out_shape=[
            jax.ShapeDtypeStruct(weights.shape, jnp.float32),
            jax.ShapeDtypeStruct((8, 512), jnp.float32),
        ],
        compiler_params=pltpu.CompilerParams(vmem_limit_bytes=VMEM_LIMIT),
        name="adam",
    )(step_index, all_squares, *pieces, weights, first, second)


def moments_kernel(clip, *refs):
    *pieces, first, second, new_first, new_second = refs
    row = 0
    for piece in pieces:
        rows = pl.ds(row, piece.shape[0])
        row += piece.shape[0]
        clipped = clip[:1] * piece[...]
        new_first[rows] = BETA_ONE * first[rows] + (1.0 - BETA_ONE) * clipped
        new_second[rows] = BETA_TWO * second[rows] + (1.0 - BETA_TWO) * clipped * clipped


def moments(clip, pieces, first, second):
    vmem = pl.BlockSpec(memory_space=pltpu.VMEM)
    return pl.pallas_call(
        moments_kernel,
        in_specs=[vmem] * (len(pieces) + 3),
        out_specs=[vmem] * 2,
        out_shape=[jax.ShapeDtypeStruct(first.shape, jnp.float32)] * 2,
        cost_estimate=pl.CostEstimate(
            flops=8 * first.size, bytes_accessed=20 * first.size, transcendentals=0
        ),
        compiler_params=pltpu.CompilerParams(vmem_limit_bytes=VMEM_LIMIT),
        name="moments",
    )(clip, *pieces, first, second)


def finish(apart, packed, updated, clip, pieces, first, second):
    theirs = from_partner(apart, packed)
    new_first, new_second = moments(clip, pieces, first, second)
    new_weights = 0.5 * (updated + theirs.astype(jnp.float32))
    return new_weights, new_first, new_second


def local(tokens, key_grads, weights, first_moment, second_moment, step_index):
    inputs = tokens[0]
    grads_out = key_grads[0]
    me = lax.axis_index("fsdp")[None]

    source = (me, step_index, inputs, grads_out)
    (corner_out,) = fetch(me, inputs, grads_out, ((CORNER, 1),), (1024,))
    theirs_corner = exchange(corner_out, 0)
    far_out, mine_corner = fetch(
        me, inputs, grads_out, ((FAR, 1), (CORNER, 0)), (1536, 1024)
    )
    theirs_far = exchange(far_out, 0)
    grads_pair = (mine_corner, theirs_corner)
    acc_corner, _, mine_far = product(
        *source, mine_corner, theirs_corner, *grads_pair, 1, ((FAR, 0),), (1536,)
    )

    def own(d, row, rows):
        acc, slot = (acc_far, FAR.index(d)) if d in FAR else (acc_near, NEAR.index(d))
        return acc[slot, row : row + rows] * SEND_SCALE

    def pack(array):
        return array.astype(jnp.float16)

    parts = {dim: [p for at in range(3) for p in PARTS if p[2][at] == dim] for dim in (X, A, B)}
    packed = {}
    for dim in (X, A, B):
        row, rows, _ = parts[dim][0]
        packed[dim] = pack(acc_corner[0, row : row + rows] * SEND_SCALE)
    corner = {dim: exchange(packed[dim], dim) for dim in packed}
    mine_far, _ = lax.optimization_barrier((mine_far, packed))
    acc_far, level, near_out, mine_near = product(
        *source, mine_far, theirs_far, *grads_pair, 3, ((NEAR, 1), (NEAR, 0)), (2048, 2048)
    )
    theirs_near = exchange(near_out, 0)
    acc_near, _ = product(*source, mine_near, theirs_near, *grads_pair, 4, (), ())
    for dim in (X, A, B):
        row, rows, _ = parts[dim][0]
        packed[dim] = pack(acc_far[PAIR[dim][0], row : row + rows] * SEND_SCALE)
    pairs = {dim: exchange(packed[dim], dim) for dim in packed}

    def from_pair(dim, d):
        return pairs[dim][PAIR[dim][1].index(d)].astype(jnp.float32)

    for dim in (X, A, B):
        row, rows, (e1, e2, e3) = parts[dim][1]
        packed[dim] = pack(own(e2 | e3, row, rows) + corner[e1].astype(jnp.float32))
    ahead = {dim: exchange(packed[dim], dim) for dim in packed}
    for dim in (X, A, B):
        row, rows, _ = parts[dim][0]
        packed[dim] = pack(own(dim, row, rows))
    lasts = {dim: exchange(packed[dim], dim) for dim in packed}
    acc_near, _ = lax.optimization_barrier((acc_near, packed))
    for dim in (X, A, B):
        row, rows, (e1, e2, e3) = parts[dim][1]
        packed[dim] = pack(own(e2, row, rows) + from_pair(e1, e1 | e2))
    behinds = {dim: exchange(packed[dim], dim) for dim in packed}
    acc_near, _ = lax.optimization_barrier((acc_near, packed))
    for dim in (X, A, B):
        row, rows, (e1, e2, e3) = parts[dim][2]
        packed[dim] = pack(
            own(e3, row, rows) + from_pair(e1, e1 | e3) + ahead[e2].astype(jnp.float32)
        )
    thirds = {dim: exchange(packed[dim], dim) for dim in packed}
    acc_near, weights, first_moment, second_moment, _ = lax.optimization_barrier(
        (acc_near, weights[0], first_moment[0], second_moment[0], packed)
    )
    weights, first_moment, second_moment = hold(weights, first_moment, second_moment)
    acc_near, weights, first_moment, second_moment = lax.optimization_barrier(
        (acc_near, weights, first_moment, second_moment)
    )
    pieces = [
        own(0, row, rows)
        + lasts[e1].astype(jnp.float32)
        + behinds[e2].astype(jnp.float32)
        + thirds[e3].astype(jnp.float32)
        for row, rows, (e1, e2, e3) in PARTS
    ]

    all_squares = lax.all_to_all(squares_of(pieces), "fsdp", 0, 0, tiled=True)
    updated, clip = adam(step_index, all_squares, pieces, weights, first_moment, second_moment)
    outs = conditionals._switch_internal(
        level[0],
        [partial(finish, apart) for apart in range(4)],
        (pack(updated), updated, clip, pieces, first_moment, second_moment),
        branches_platforms=None,
    )
    return tuple(out[None] for out in outs)


def solution(mesh):
    spec = P("replica", "fsdp", None)
    return jax.shard_map(
        local,
        mesh=mesh,
        in_specs=(spec, spec, spec, spec, spec, P()),
        out_specs=(spec, spec, spec),
        check_vma=False,
    )
```

```python
from functools import partial
import math

import jax
import jax.numpy as jnp
from jax import lax
from jax._src.lax.control_flow import conditionals
from jax.experimental import pallas as pl
from jax.experimental.pallas import tpu as pltpu
from jax.sharding import PartitionSpec as P


BETA_ONE = 0.9
BETA_TWO = 0.95
LEARN_RATE = 0.08
ADAM_EPS = 1e-08
NORM_EPS = 1e-06

FIRST_SCALE, SECOND_SCALE, THIRD_SCALE = 2.0**-5, 2.0**-6, 2.0**-7

X, A, B = 1, 2, 4
PARTS = ((0, 176, (X, A, B)), (176, 176, (A, B, X)), (352, 160, (B, X, A)))


def neighbour(i, dim):
    y, x, c = i >> 2, (i >> 1) & 1, i & 1
    g = y ^ (y >> 1)
    if dim == X:
        x ^= 1
    elif dim == A:
        g ^= 1
    elif dim == B:
        g ^= 2
    else:
        c ^= 1
    y = g ^ (g >> 1)
    return (y << 2) | (x << 1) | c


def exchange(array, dim):
    return lax.ppermute(array, "fsdp", [(i, neighbour(i, dim)) for i in range(16)])


def from_partner(apart, array):
    return lax.ppermute(array, "replica", [(i, i ^ 1 << apart) for i in range(16)])


def block_of(me, d, flip):
    y, x, c = me >> 2, (me >> 1) & 1, me & 1
    g = (y ^ (y >> 1)) ^ (d >> 1)
    return ((g ^ (g >> 1)) << 2) | ((x ^ (d & 1)) << 1) | (c ^ flip)


CORNER = (7,)
FAR = (5, 3, 6)
NEAR = (1, 2, 4, 0)
PAIR = {X: (slice(0, 2), (5, 3)), A: (slice(1, 3), (3, 6)), B: (slice(0, 3, 2), (5, 6))}
VMEM_LIMIT = 24 << 20


def start_fetch(wanted, me, tokens, grads, outs, sems):
    copies = []
    for out, (order, flip) in zip(outs, wanted):
        for j, d in enumerate(order):
            column = pl.multiple_of(block_of(me[0], d, flip) * 512, 512)
            copies.append(
                pltpu.make_async_copy(
                    tokens.at[:, pl.ds(column, 512)],
                    out.at[:, pl.ds(j * 512, 512)],
                    sems.at[len(copies)],
                )
            )
        if out.shape[1] > 512 * len(order):
            copies.append(
                pltpu.make_async_copy(
                    grads, out.at[:, pl.ds(512 * len(order), 512)], sems.at[len(copies)]
                )
            )
    for copy in copies:
        copy.start()
    return copies


def fetch_kernel(wanted, me, tokens, grads, *refs):
    *outs, sems = refs
    for copy in start_fetch(wanted, me, tokens, grads, outs, sems):
        copy.wait()


def fetch(me, tokens, grads, wanted, widths):
    t = tokens.shape[0]
    return pl.pallas_call(
        partial(fetch_kernel, wanted),
        in_specs=[
            pl.BlockSpec(memory_space=pltpu.SMEM),
            pl.BlockSpec(memory_space=pltpu.HBM),
            pl.BlockSpec(memory_space=pltpu.HBM),
        ],
        out_shape=[pltpu.VMEM((t, width), tokens.dtype) for width in widths],
        scratch_shapes=[pltpu.SemaphoreType.DMA((8,))],
        cost_estimate=pl.CostEstimate(
            flops=0, bytes_accessed=4 * t * sum(widths), transcendentals=0
        ),
        compiler_params=pltpu.CompilerParams(vmem_limit_bytes=VMEM_LIMIT),
        name="fetch",
    )(
        me,
        pltpu.with_memory_space_constraint(tokens, pltpu.HBM),
        pltpu.with_memory_space_constraint(grads, pltpu.HBM),
    )


def hold_kernel(step_index, *refs):
    *pairs, level, sems = refs
    level[0] = step_index[0] % 4
    n = len(pairs) // 2
    copies = [pltpu.make_async_copy(pairs[i], pairs[n + i], sems.at[i]) for i in range(n)]
    for copy in copies:
        copy.start()
    for copy in copies:
        copy.wait()


def hold(step_index, *arrays):
    return pl.pallas_call(
        hold_kernel,
        in_specs=[pl.BlockSpec(memory_space=pltpu.SMEM)]
        + [pl.BlockSpec(memory_space=pltpu.HBM)] * len(arrays),
        out_specs=[pl.BlockSpec(memory_space=pltpu.VMEM)] * len(arrays)
        + [pl.BlockSpec(memory_space=pltpu.SMEM)],
        out_shape=[pltpu.VMEM(a.shape, a.dtype) for a in arrays]
        + [jax.ShapeDtypeStruct((1,), jnp.int32)],
        scratch_shapes=[pltpu.SemaphoreType.DMA((len(arrays),))],
        compiler_params=pltpu.CompilerParams(vmem_limit_bytes=VMEM_LIMIT),
        name="hold",
    )(step_index, *[pltpu.with_memory_space_constraint(a, pltpu.HBM) for a in arrays])


def product_kernel(wanted, me, tokens, grads, mine, theirs, g_mine, g_theirs, *refs):
    out, *outs, both_tokens, both_grads, sems = refs
    t = g_mine.shape[0]
    copies = start_fetch(wanted, me, tokens, grads, outs, sems)
    both_grads[:t] = g_mine[:, 512:]
    both_grads[t:] = g_theirs[:, 512:]

    def block(j, _):
        column = pl.multiple_of(j * 512, 512)
        both_tokens[:t] = mine[:, pl.ds(column, 512)]
        both_tokens[t:] = theirs[:, pl.ds(column, 512)]
        out[j] = lax.dot_general(
            both_tokens[...],
            both_grads[...],
            (((0,), (0,)), ((), ())),
            preferred_element_type=jnp.float32,
        )
        return _

    lax.fori_loop(0, out.shape[0], block, None)
    for copy in copies:
        copy.wait()


def product(me, tokens, grads, mine, theirs, g_mine, g_theirs, blocks, wanted, widths):
    t, k = g_mine.shape[0], 512
    vmem = pl.BlockSpec(memory_space=pltpu.VMEM)
    smem = pl.BlockSpec(memory_space=pltpu.SMEM)
    hbm = pl.BlockSpec(memory_space=pltpu.HBM)
    return pl.pallas_call(
        partial(product_kernel, wanted),
        in_specs=[smem, hbm, hbm] + [vmem] * 4,
        out_specs=[vmem] * (1 + len(wanted)),
        scratch_shapes=[
            pltpu.VMEM((2 * t, 512), mine.dtype),
            pltpu.VMEM((2 * t, k), mine.dtype),
            pltpu.SemaphoreType.DMA((8,)),
        ],
        out_shape=[pltpu.VMEM((blocks, 512, k), jnp.float32)]
        + [pltpu.VMEM((t, width), tokens.dtype) for width in widths],
        cost_estimate=pl.CostEstimate(
            flops=4 * t * 512 * blocks * k, bytes_accessed=4 * t * sum(widths), transcendentals=0
        ),
        compiler_params=pltpu.CompilerParams(vmem_limit_bytes=VMEM_LIMIT),
        name="product",
    )(
        me,
        pltpu.with_memory_space_constraint(tokens, pltpu.HBM),
        pltpu.with_memory_space_constraint(grads, pltpu.HBM),
        mine,
        theirs,
        g_mine,
        g_theirs,
    )


def squares_kernel(*refs):
    *pieces, out = refs
    total = sum(jnp.sum((p[...] * p[...]).reshape(-1, 8, 512), axis=0) for p in pieces)
    total = total[:, :128] + total[:, 128:256] + total[:, 256:384] + total[:, 384:]
    total = jnp.sum(total, axis=0, keepdims=True)
    out[...] = jnp.broadcast_to(total[None], out.shape)


def squares_of(pieces):
    return pl.pallas_call(
        squares_kernel,
        out_shape=jax.ShapeDtypeStruct((16, 1, 128), jnp.float32),
        compiler_params=pltpu.CompilerParams(vmem_limit_bytes=VMEM_LIMIT),
        name="squares",
    )(*pieces)


def adam_kernel(step_index, all_squares, *refs):
    *pieces, weights, first, second, updated, clip_out = refs
    squares = jnp.sum(all_squares[...], axis=0)
    squares = jnp.sum(squares, axis=1, keepdims=True)
    norm = jnp.sqrt(squares)
    clip = jnp.minimum(1.0, math.sqrt(8192 * 512) / (norm + NORM_EPS))
    clip_out[...] = jnp.broadcast_to(clip, clip_out.shape)
    steps = jnp.full((1, 1), step_index[0] + 1, jnp.int32).astype(jnp.float32)
    rate = LEARN_RATE / (1.0 - jnp.exp(steps * math.log(BETA_ONE)))
    second_scale = 1.0 / (1.0 - jnp.exp(steps * math.log(BETA_TWO)))
    row = 0
    for piece in pieces:
        rows = pl.ds(row, piece.shape[0])
        row += piece.shape[0]
        clipped = clip * piece[...]
        one = BETA_ONE * first[rows] + (1.0 - BETA_ONE) * clipped
        two = BETA_TWO * second[rows] + (1.0 - BETA_TWO) * clipped * clipped
        updated[rows] = weights[rows] - rate * one / (jnp.sqrt(two * second_scale) + ADAM_EPS)


def adam(step_index, all_squares, pieces, weights, first, second):
    vmem = pl.BlockSpec(memory_space=pltpu.VMEM)
    return pl.pallas_call(
        adam_kernel,
        in_specs=[pl.BlockSpec(memory_space=pltpu.SMEM)] + [vmem] * (len(pieces) + 4),
        out_specs=[vmem] * 2,
        out_shape=[
            jax.ShapeDtypeStruct(weights.shape, jnp.float32),
            jax.ShapeDtypeStruct((8, 512), jnp.float32),
        ],
        compiler_params=pltpu.CompilerParams(vmem_limit_bytes=VMEM_LIMIT),
        name="adam",
    )(step_index, all_squares, *pieces, weights, first, second)


def moments_kernel(clip, *refs):
    *pieces, first, second, new_first, new_second = refs
    row = 0
    for piece in pieces:
        rows = pl.ds(row, piece.shape[0])
        row += piece.shape[0]
        clipped = clip[:1] * piece[...]
        new_first[rows] = BETA_ONE * first[rows] + (1.0 - BETA_ONE) * clipped
        new_second[rows] = BETA_TWO * second[rows] + (1.0 - BETA_TWO) * clipped * clipped


def moments(clip, pieces, first, second):
    vmem = pl.BlockSpec(memory_space=pltpu.VMEM)
    return pl.pallas_call(
        moments_kernel,
        in_specs=[vmem] * (len(pieces) + 3),
        out_specs=[vmem] * 2,
        out_shape=[jax.ShapeDtypeStruct(first.shape, jnp.float32)] * 2,
        cost_estimate=pl.CostEstimate(
            flops=8 * first.size, bytes_accessed=20 * first.size, transcendentals=0
        ),
        compiler_params=pltpu.CompilerParams(vmem_limit_bytes=VMEM_LIMIT),
        name="moments",
    )(clip, *pieces, first, second)


def finish(apart, packed, updated, clip, pieces, first, second):
    theirs = from_partner(apart, packed)
    new_first, new_second = moments(clip, pieces, first, second)
    new_weights = 0.5 * (updated + theirs.astype(jnp.float32))
    return new_weights, new_first, new_second


def local(tokens, key_grads, weights, first_moment, second_moment, step_index):
    inputs = tokens[0]
    grads_out = key_grads[0]
    me = lax.axis_index("fsdp")[None]

    source = (me, inputs, grads_out)
    (corner_out,) = fetch(me, inputs, grads_out, ((CORNER, 1),), (1024,))
    theirs_corner = exchange(corner_out, 0)
    far_out, mine_corner = fetch(
        me, inputs, grads_out, ((FAR, 1), (CORNER, 0)), (1536, 1024)
    )
    theirs_far = exchange(far_out, 0)
    grads_pair = (mine_corner, theirs_corner)
    acc_corner, mine_far = product(
        *source, mine_corner, theirs_corner, *grads_pair, 1, ((FAR, 0),), (1536,)
    )

    def own(d, row, rows):
        acc, slot = (acc_far, FAR.index(d)) if d in FAR else (acc_near, NEAR.index(d))
        return acc[slot, row : row + rows]

    def pack(array, scale=1.0):
        return (array * scale).astype(jnp.float16)

    def unpack(message, scale):
        return message.astype(jnp.float32) * (1.0 / scale)

    parts = {dim: [p for at in range(3) for p in PARTS if p[2][at] == dim] for dim in (X, A, B)}
    packed = {}
    for dim in (X, A, B):
        row, rows, _ = parts[dim][0]
        packed[dim] = pack(acc_corner[0, row : row + rows], FIRST_SCALE)
    corner = {dim: exchange(packed[dim], dim) for dim in packed}
    mine_far, _ = lax.optimization_barrier((mine_far, packed))
    acc_far, near_out, mine_near = product(
        *source, mine_far, theirs_far, *grads_pair, 3, ((NEAR, 1), (NEAR, 0)), (2048, 2048)
    )
    theirs_near = exchange(near_out, 0)
    (acc_near,) = product(*source, mine_near, theirs_near, *grads_pair, 4, (), ())
    for dim in (X, A, B):
        row, rows, _ = parts[dim][0]
        packed[dim] = pack(acc_far[PAIR[dim][0], row : row + rows], FIRST_SCALE)
    pairs = {dim: exchange(packed[dim], dim) for dim in packed}

    def from_pair(dim, d):
        return unpack(pairs[dim][PAIR[dim][1].index(d)], FIRST_SCALE)

    for dim in (X, A, B):
        row, rows, (e1, e2, e3) = parts[dim][1]
        packed[dim] = pack(
            own(e2 | e3, row, rows) + unpack(corner[e1], FIRST_SCALE), SECOND_SCALE
        )
    ahead = {dim: exchange(packed[dim], dim) for dim in packed}
    for dim in (X, A, B):
        row, rows, _ = parts[dim][0]
        packed[dim] = pack(own(dim, row, rows), FIRST_SCALE)
    lasts = {dim: exchange(packed[dim], dim) for dim in packed}
    acc_near, _ = lax.optimization_barrier((acc_near, packed))
    for dim in (X, A, B):
        row, rows, (e1, e2, e3) = parts[dim][1]
        packed[dim] = pack(own(e2, row, rows) + from_pair(e1, e1 | e2), SECOND_SCALE)
    behinds = {dim: exchange(packed[dim], dim) for dim in packed}
    acc_near, _ = lax.optimization_barrier((acc_near, packed))
    for dim in (X, A, B):
        row, rows, (e1, e2, e3) = parts[dim][2]
        packed[dim] = pack(
            own(e3, row, rows) + from_pair(e1, e1 | e3) + unpack(ahead[e2], SECOND_SCALE),
            THIRD_SCALE,
        )
    thirds = {dim: exchange(packed[dim], dim) for dim in packed}
    acc_near, weights, first_moment, second_moment, _ = lax.optimization_barrier(
        (acc_near, weights[0], first_moment[0], second_moment[0], packed)
    )
    weights, first_moment, second_moment, level = hold(
        step_index, weights, first_moment, second_moment
    )
    acc_near, weights, first_moment, second_moment = lax.optimization_barrier(
        (acc_near, weights, first_moment, second_moment)
    )
    pieces = [
        own(0, row, rows)
        + unpack(lasts[e1], FIRST_SCALE)
        + unpack(behinds[e2], SECOND_SCALE)
        + unpack(thirds[e3], THIRD_SCALE)
        for row, rows, (e1, e2, e3) in PARTS
    ]

    all_squares = lax.all_to_all(squares_of(pieces), "fsdp", 0, 0, tiled=True)
    updated, clip = adam(step_index, all_squares, pieces, weights, first_moment, second_moment)
    outs = conditionals._switch_internal(
        level[0],
        [partial(finish, apart) for apart in range(4)],
        (pack(updated), updated, clip, pieces, first_moment, second_moment),
        branches_platforms=None,
    )
    return tuple(out[None] for out in outs)


def solution(mesh):
    spec = P("replica", "fsdp", None)
    return jax.shard_map(
        local,
        mesh=mesh,
        in_specs=(spec, spec, spec, spec, spec, P()),
        out_specs=(spec, spec, spec),
        check_vma=False,
    )
```

```python
from functools import partial
import math

import jax
import jax.numpy as jnp
from jax import lax
from jax._src.lax.control_flow import conditionals
from jax.experimental import pallas as pl
from jax.experimental.pallas import tpu as pltpu
from jax.sharding import PartitionSpec as P


BETA_ONE = 0.9
BETA_TWO = 0.95
LEARN_RATE = 0.08
ADAM_EPS = 1e-08
NORM_EPS = 1e-06

FIRST_SCALE, SECOND_SCALE, THIRD_SCALE = 2.0**-5, 2.0**-6, 2.0**-7

X, A, B = 1, 2, 4
PARTS = ((0, 176, (X, A, B)), (176, 176, (A, B, X)), (352, 160, (B, X, A)))


def neighbour(i, dim):
    y, x, c = i >> 2, (i >> 1) & 1, i & 1
    g = y ^ (y >> 1)
    if dim == X:
        x ^= 1
    elif dim == A:
        g ^= 1
    elif dim == B:
        g ^= 2
    else:
        c ^= 1
    y = g ^ (g >> 1)
    return (y << 2) | (x << 1) | c


def exchange(array, dim):
    return lax.ppermute(array, "fsdp", [(i, neighbour(i, dim)) for i in range(16)])


def from_partner(apart, array):
    return lax.ppermute(array, "replica", [(i, i ^ 1 << apart) for i in range(16)])


def block_of(me, d, flip):
    y, x, c = me >> 2, (me >> 1) & 1, me & 1
    g = (y ^ (y >> 1)) ^ (d >> 1)
    return ((g ^ (g >> 1)) << 2) | ((x ^ (d & 1)) << 1) | (c ^ flip)


CORNER = (7,)
FAR = (5, 3, 6)
NEAR = (1, 2, 4, 0)
PAIR = {X: (slice(0, 2), (5, 3)), A: (slice(1, 3), (3, 6)), B: (slice(0, 3, 2), (5, 6))}
VMEM_LIMIT = 24 << 20


def start_fetch(wanted, me, tokens, grads, outs, sems):
    copies = []
    for out, (order, flip) in zip(outs, wanted):
        for j, d in enumerate(order):
            column = pl.multiple_of(block_of(me[0], d, flip) * 512, 512)
            copies.append(
                pltpu.make_async_copy(
                    tokens.at[:, pl.ds(column, 512)],
                    out.at[:, pl.ds(j * 512, 512)],
                    sems.at[len(copies)],
                )
            )
        if out.shape[1] > 512 * len(order):
            copies.append(
                pltpu.make_async_copy(
                    grads, out.at[:, pl.ds(512 * len(order), 512)], sems.at[len(copies)]
                )
            )
    for copy in copies:
        copy.start()
    return copies


def fetch_kernel(wanted, me, tokens, grads, *refs):
    *outs, sems = refs
    for copy in start_fetch(wanted, me, tokens, grads, outs, sems):
        copy.wait()


def fetch(me, tokens, grads, wanted, widths):
    t = tokens.shape[0]
    return pl.pallas_call(
        partial(fetch_kernel, wanted),
        in_specs=[
            pl.BlockSpec(memory_space=pltpu.SMEM),
            pl.BlockSpec(memory_space=pltpu.HBM),
            pl.BlockSpec(memory_space=pltpu.HBM),
        ],
        out_shape=[pltpu.VMEM((t, width), tokens.dtype) for width in widths],
        scratch_shapes=[pltpu.SemaphoreType.DMA((8,))],
        cost_estimate=pl.CostEstimate(
            flops=0, bytes_accessed=4 * t * sum(widths), transcendentals=0
        ),
        compiler_params=pltpu.CompilerParams(vmem_limit_bytes=VMEM_LIMIT),
        name="fetch",
    )(
        me,
        pltpu.with_memory_space_constraint(tokens, pltpu.HBM),
        pltpu.with_memory_space_constraint(grads, pltpu.HBM),
    )


def hold_kernel(step_index, *refs):
    *pairs, level, sems = refs
    level[0] = step_index[0] % 4
    n = len(pairs) // 2
    copies = [pltpu.make_async_copy(pairs[i], pairs[n + i], sems.at[i]) for i in range(n)]
    for copy in copies:
        copy.start()
    for copy in copies:
        copy.wait()


def hold(step_index, *arrays):
    return pl.pallas_call(
        hold_kernel,
        in_specs=[pl.BlockSpec(memory_space=pltpu.SMEM)]
        + [pl.BlockSpec(memory_space=pltpu.HBM)] * len(arrays),
        out_specs=[pl.BlockSpec(memory_space=pltpu.VMEM)] * len(arrays)
        + [pl.BlockSpec(memory_space=pltpu.SMEM)],
        out_shape=[pltpu.VMEM(a.shape, a.dtype) for a in arrays]
        + [jax.ShapeDtypeStruct((1,), jnp.int32)],
        scratch_shapes=[pltpu.SemaphoreType.DMA((len(arrays),))],
        compiler_params=pltpu.CompilerParams(vmem_limit_bytes=VMEM_LIMIT),
        name="hold",
    )(step_index, *[pltpu.with_memory_space_constraint(a, pltpu.HBM) for a in arrays])


def product_kernel(wanted, me, tokens, grads, mine, theirs, g_mine, g_theirs, *refs):
    out, *outs, both_tokens, both_grads, sems = refs
    t = g_mine.shape[0]
    copies = start_fetch(wanted, me, tokens, grads, outs, sems)
    both_grads[:t] = g_mine[:, 512:]
    both_grads[t:] = g_theirs[:, 512:]

    def block(j, _):
        column = pl.multiple_of(j * 512, 512)
        both_tokens[:t] = mine[:, pl.ds(column, 512)]
        both_tokens[t:] = theirs[:, pl.ds(column, 512)]
        out[j] = lax.dot_general(
            both_tokens[...],
            both_grads[...],
            (((0,), (0,)), ((), ())),
            preferred_element_type=jnp.float32,
        )
        return _

    lax.fori_loop(0, out.shape[0], block, None)
    for copy in copies:
        copy.wait()


def product(me, tokens, grads, mine, theirs, g_mine, g_theirs, blocks, wanted, widths):
    t, k = g_mine.shape[0], 512
    vmem = pl.BlockSpec(memory_space=pltpu.VMEM)
    smem = pl.BlockSpec(memory_space=pltpu.SMEM)
    hbm = pl.BlockSpec(memory_space=pltpu.HBM)
    return pl.pallas_call(
        partial(product_kernel, wanted),
        in_specs=[smem, hbm, hbm] + [vmem] * 4,
        out_specs=[vmem] * (1 + len(wanted)),
        scratch_shapes=[
            pltpu.VMEM((2 * t, 512), mine.dtype),
            pltpu.VMEM((2 * t, k), mine.dtype),
            pltpu.SemaphoreType.DMA((8,)),
        ],
        out_shape=[pltpu.VMEM((blocks, 512, k), jnp.float32)]
        + [pltpu.VMEM((t, width), tokens.dtype) for width in widths],
        cost_estimate=pl.CostEstimate(
            flops=4 * t * 512 * blocks * k, bytes_accessed=4 * t * sum(widths), transcendentals=0
        ),
        compiler_params=pltpu.CompilerParams(vmem_limit_bytes=VMEM_LIMIT),
        name="product",
    )(
        me,
        pltpu.with_memory_space_constraint(tokens, pltpu.HBM),
        pltpu.with_memory_space_constraint(grads, pltpu.HBM),
        mine,
        theirs,
        g_mine,
        g_theirs,
    )


def squares_kernel(*refs):
    *pieces, out = refs
    total = sum(jnp.sum((p[...] * p[...]).reshape(-1, 8, 512), axis=0) for p in pieces)
    total = total[:, :128] + total[:, 128:256] + total[:, 256:384] + total[:, 384:]
    total = jnp.sum(total, axis=0, keepdims=True)
    out[...] = jnp.broadcast_to(total[None], out.shape)


def squares_of(pieces):
    return pl.pallas_call(
        squares_kernel,
        out_shape=jax.ShapeDtypeStruct((16, 1, 128), jnp.float32),
        compiler_params=pltpu.CompilerParams(vmem_limit_bytes=VMEM_LIMIT),
        name="squares",
    )(*pieces)


def adam_kernel(start, step_index, all_squares, *refs):
    *pieces, weights, first, second, updated, clip_out = refs
    squares = jnp.sum(all_squares[...], axis=0)
    squares = jnp.sum(squares, axis=1, keepdims=True)
    norm = jnp.sqrt(squares)
    clip = jnp.minimum(1.0, math.sqrt(8192 * 512) / (norm + NORM_EPS))
    clip_out[...] = jnp.broadcast_to(clip, clip_out.shape)
    steps = jnp.full((1, 1), step_index[0] + 1, jnp.int32).astype(jnp.float32)
    rate = LEARN_RATE / (1.0 - jnp.exp(steps * math.log(BETA_ONE)))
    second_scale = 1.0 / (1.0 - jnp.exp(steps * math.log(BETA_TWO)))
    row = start
    for piece in pieces:
        rows = pl.ds(row, piece.shape[0])
        mine = pl.ds(row - start, piece.shape[0])
        row += piece.shape[0]
        clipped = clip * piece[...]
        one = BETA_ONE * first[rows] + (1.0 - BETA_ONE) * clipped
        two = BETA_TWO * second[rows] + (1.0 - BETA_TWO) * clipped * clipped
        updated[mine] = weights[rows] - rate * one / (jnp.sqrt(two * second_scale) + ADAM_EPS)


def adam(start, step_index, all_squares, pieces, weights, first, second):
    vmem = pl.BlockSpec(memory_space=pltpu.VMEM)
    return pl.pallas_call(
        partial(adam_kernel, start),
        in_specs=[pl.BlockSpec(memory_space=pltpu.SMEM)] + [vmem] * (len(pieces) + 4),
        out_specs=[vmem] * 2,
        out_shape=[
            jax.ShapeDtypeStruct((sum(p.shape[0] for p in pieces), 512), jnp.float32),
            jax.ShapeDtypeStruct((8, 512), jnp.float32),
        ],
        cost_estimate=pl.CostEstimate(
            flops=20 * 512 * 512, bytes_accessed=16 * 512 * 512, transcendentals=512 * 512
        ),
        compiler_params=pltpu.CompilerParams(vmem_limit_bytes=VMEM_LIMIT),
        name="adam",
    )(step_index, all_squares, *pieces, weights, first, second)


def moments_kernel(clip, *refs):
    *pieces, first, second, new_first, new_second = refs
    row = 0
    for piece in pieces:
        rows = pl.ds(row, piece.shape[0])
        row += piece.shape[0]
        clipped = clip[:1] * piece[...]
        new_first[rows] = BETA_ONE * first[rows] + (1.0 - BETA_ONE) * clipped
        new_second[rows] = BETA_TWO * second[rows] + (1.0 - BETA_TWO) * clipped * clipped


def moments(clip, pieces, first, second):
    vmem = pl.BlockSpec(memory_space=pltpu.VMEM)
    return pl.pallas_call(
        moments_kernel,
        in_specs=[vmem] * (len(pieces) + 3),
        out_specs=[vmem] * 2,
        out_shape=[jax.ShapeDtypeStruct(first.shape, jnp.float32)] * 2,
        cost_estimate=pl.CostEstimate(
            flops=8 * first.size, bytes_accessed=20 * first.size, transcendentals=0
        ),
        compiler_params=pltpu.CompilerParams(vmem_limit_bytes=VMEM_LIMIT),
        name="moments",
    )(clip, *pieces, first, second)


def finish(apart, packed, updated, clip, pieces, weights, first, second, step_index, all_squares):
    f32 = jnp.float32
    theirs = from_partner(apart, packed)
    start = packed.shape[0]
    behind, _ = adam(start, step_index, all_squares, pieces[1:], weights, first, second)
    theirs_behind = from_partner(apart, behind.astype(jnp.float16))
    new_first, new_second = moments(clip, pieces, first, second)
    new_weights = jnp.concatenate(
        [0.5 * (updated + theirs.astype(f32)), 0.5 * (behind + theirs_behind.astype(f32))]
    )
    return new_weights, new_first, new_second


def local(tokens, key_grads, weights, first_moment, second_moment, step_index):
    inputs = tokens[0]
    grads_out = key_grads[0]
    me = lax.axis_index("fsdp")[None]

    source = (me, inputs, grads_out)
    (corner_out,) = fetch(me, inputs, grads_out, ((CORNER, 1),), (1024,))
    theirs_corner = exchange(corner_out, 0)
    far_out, mine_corner, mine_far = fetch(
        me, inputs, grads_out, ((FAR, 1), (CORNER, 0), (FAR, 0)), (1536, 1024, 1536)
    )
    theirs_far = exchange(far_out, 0)
    grads_pair = (mine_corner, theirs_corner)
    (acc_corner,) = product(*source, mine_corner, theirs_corner, *grads_pair, 1, (), ())

    def own(d, row, rows):
        acc, slot = (acc_far, FAR.index(d)) if d in FAR else (acc_near, NEAR.index(d))
        return acc[slot, row : row + rows]

    def pack(array, scale=1.0):
        return (array * scale).astype(jnp.float16)

    def unpack(message, scale):
        return message.astype(jnp.float32) * (1.0 / scale)

    parts = {dim: [p for at in range(3) for p in PARTS if p[2][at] == dim] for dim in (X, A, B)}
    packed = {}
    for dim in (X, A, B):
        row, rows, _ = parts[dim][0]
        packed[dim] = pack(acc_corner[0, row : row + rows], FIRST_SCALE)
    corner = {dim: exchange(packed[dim], dim) for dim in packed}
    mine_far, _ = lax.optimization_barrier((mine_far, packed))
    acc_far, near_out, mine_near = product(
        *source, mine_far, theirs_far, *grads_pair, 3, ((NEAR, 1), (NEAR, 0)), (2048, 2048)
    )
    theirs_near = exchange(near_out, 0)
    (acc_near,) = product(*source, mine_near, theirs_near, *grads_pair, 4, (), ())
    for dim in (X, A, B):
        row, rows, _ = parts[dim][0]
        packed[dim] = pack(acc_far[PAIR[dim][0], row : row + rows], FIRST_SCALE)
    pairs = {dim: exchange(packed[dim], dim) for dim in packed}

    def from_pair(dim, d):
        return unpack(pairs[dim][PAIR[dim][1].index(d)], FIRST_SCALE)

    for dim in (X, A, B):
        row, rows, (e1, e2, e3) = parts[dim][1]
        packed[dim] = pack(
            own(e2 | e3, row, rows) + unpack(corner[e1], FIRST_SCALE), SECOND_SCALE
        )
    ahead = {dim: exchange(packed[dim], dim) for dim in packed}
    for dim in (X, A, B):
        row, rows, _ = parts[dim][0]
        packed[dim] = pack(own(dim, row, rows), FIRST_SCALE)
    lasts = {dim: exchange(packed[dim], dim) for dim in packed}
    acc_near, _ = lax.optimization_barrier((acc_near, packed))
    for dim in (X, A, B):
        row, rows, (e1, e2, e3) = parts[dim][1]
        packed[dim] = pack(own(e2, row, rows) + from_pair(e1, e1 | e2), SECOND_SCALE)
    behinds = {dim: exchange(packed[dim], dim) for dim in packed}
    acc_near, _ = lax.optimization_barrier((acc_near, packed))
    for dim in (X, A, B):
        row, rows, (e1, e2, e3) = parts[dim][2]
        packed[dim] = pack(
            own(e3, row, rows) + from_pair(e1, e1 | e3) + unpack(ahead[e2], SECOND_SCALE),
            THIRD_SCALE,
        )
    thirds = {dim: exchange(packed[dim], dim) for dim in packed}
    acc_near, weights, first_moment, second_moment, _ = lax.optimization_barrier(
        (acc_near, weights[0], first_moment[0], second_moment[0], packed)
    )
    weights, first_moment, second_moment, level = hold(
        step_index, weights, first_moment, second_moment
    )
    acc_near, weights, first_moment, second_moment = lax.optimization_barrier(
        (acc_near, weights, first_moment, second_moment)
    )
    pieces = [
        own(0, row, rows)
        + unpack(lasts[e1], FIRST_SCALE)
        + unpack(behinds[e2], SECOND_SCALE)
        + unpack(thirds[e3], THIRD_SCALE)
        for row, rows, (e1, e2, e3) in PARTS
    ]

    all_squares = lax.all_to_all(squares_of(pieces), "fsdp", 0, 0, tiled=True)
    updated, clip = adam(
        0, step_index, all_squares, pieces[:1], weights, first_moment, second_moment
    )
    outs = conditionals._switch_internal(
        level[0],
        [partial(finish, apart) for apart in range(4)],
        (
            pack(updated),
            updated,
            clip,
            pieces,
            weights,
            first_moment,
            second_moment,
            step_index,
            all_squares,
        ),
        branches_platforms=None,
    )
    return tuple(out[None] for out in outs)


def solution(mesh):
    spec = P("replica", "fsdp", None)
    return jax.shard_map(
        local,
        mesh=mesh,
        in_specs=(spec, spec, spec, spec, spec, P()),
        out_specs=(spec, spec, spec),
        check_vma=False,
    )
```

```python
from functools import partial
import math

import jax
import jax.numpy as jnp
from jax import lax
from jax._src.lax.control_flow import conditionals
from jax.experimental import pallas as pl
from jax.experimental.pallas import tpu as pltpu
from jax.sharding import PartitionSpec as P


BETA_ONE = 0.9
BETA_TWO = 0.95
LEARN_RATE = 0.08
ADAM_EPS = 1e-08
NORM_EPS = 1e-06

FIRST_SCALE, SECOND_SCALE, THIRD_SCALE = 2.0**-5, 2.0**-6, 2.0**-7

X, A, B = 1, 2, 4
PARTS = ((0, 176, (X, A, B)), (176, 176, (A, B, X)), (352, 160, (B, X, A)))


def neighbour(i, dim):
    y, x, c = i >> 2, (i >> 1) & 1, i & 1
    g = y ^ (y >> 1)
    if dim == X:
        x ^= 1
    elif dim == A:
        g ^= 1
    elif dim == B:
        g ^= 2
    else:
        c ^= 1
    y = g ^ (g >> 1)
    return (y << 2) | (x << 1) | c


def exchange(array, dim):
    return lax.ppermute(array, "fsdp", [(i, neighbour(i, dim)) for i in range(16)])


def from_partner(apart, array):
    return lax.ppermute(array, "replica", [(i, i ^ 1 << apart) for i in range(16)])


def block_of(me, d, flip):
    y, x, c = me >> 2, (me >> 1) & 1, me & 1
    g = (y ^ (y >> 1)) ^ (d >> 1)
    return ((g ^ (g >> 1)) << 2) | ((x ^ (d & 1)) << 1) | (c ^ flip)


CORNER = (7,)
FAR = (5, 3, 6)
NEAR = (1, 2, 4, 0)
PAIR = {X: (slice(0, 2), (5, 3)), A: (slice(1, 3), (3, 6)), B: (slice(0, 3, 2), (5, 6))}
VMEM_LIMIT = 24 << 20


def start_fetch(wanted, me, tokens, grads, outs, sems):
    copies = []
    for out, (order, flip) in zip(outs, wanted):
        for j, d in enumerate(order):
            column = pl.multiple_of(block_of(me[0], d, flip) * 512, 512)
            copies.append(
                pltpu.make_async_copy(
                    tokens.at[:, pl.ds(column, 512)],
                    out.at[:, pl.ds(j * 512, 512)],
                    sems.at[len(copies)],
                )
            )
        if out.shape[1] > 512 * len(order):
            copies.append(
                pltpu.make_async_copy(
                    grads, out.at[:, pl.ds(512 * len(order), 512)], sems.at[len(copies)]
                )
            )
    for copy in copies:
        copy.start()
    return copies


def fetch_kernel(wanted, me, tokens, grads, *refs):
    *outs, sems = refs
    for copy in start_fetch(wanted, me, tokens, grads, outs, sems):
        copy.wait()


def fetch(me, tokens, grads, wanted, widths):
    t = tokens.shape[0]
    return pl.pallas_call(
        partial(fetch_kernel, wanted),
        in_specs=[
            pl.BlockSpec(memory_space=pltpu.SMEM),
            pl.BlockSpec(memory_space=pltpu.HBM),
            pl.BlockSpec(memory_space=pltpu.HBM),
        ],
        out_shape=[pltpu.VMEM((t, width), tokens.dtype) for width in widths],
        scratch_shapes=[pltpu.SemaphoreType.DMA((8,))],
        cost_estimate=pl.CostEstimate(
            flops=0, bytes_accessed=4 * t * sum(widths), transcendentals=0
        ),
        compiler_params=pltpu.CompilerParams(vmem_limit_bytes=VMEM_LIMIT),
        name="fetch",
    )(
        me,
        pltpu.with_memory_space_constraint(tokens, pltpu.HBM),
        pltpu.with_memory_space_constraint(grads, pltpu.HBM),
    )


def hold_kernel(step_index, *refs):
    *pairs, level, sems = refs
    level[0] = step_index[0] % 4
    n = len(pairs) // 2
    copies = [pltpu.make_async_copy(pairs[i], pairs[n + i], sems.at[i]) for i in range(n)]
    for copy in copies:
        copy.start()
    for copy in copies:
        copy.wait()


def hold(step_index, *arrays):
    return pl.pallas_call(
        hold_kernel,
        in_specs=[pl.BlockSpec(memory_space=pltpu.SMEM)]
        + [pl.BlockSpec(memory_space=pltpu.HBM)] * len(arrays),
        out_specs=[pl.BlockSpec(memory_space=pltpu.VMEM)] * len(arrays)
        + [pl.BlockSpec(memory_space=pltpu.SMEM)],
        out_shape=[pltpu.VMEM(a.shape, a.dtype) for a in arrays]
        + [jax.ShapeDtypeStruct((1,), jnp.int32)],
        scratch_shapes=[pltpu.SemaphoreType.DMA((len(arrays),))],
        compiler_params=pltpu.CompilerParams(vmem_limit_bytes=VMEM_LIMIT),
        name="hold",
    )(step_index, *[pltpu.with_memory_space_constraint(a, pltpu.HBM) for a in arrays])


def product_kernel(wanted, me, tokens, grads, mine, theirs, g_mine, g_theirs, *refs):
    out, *outs, both_tokens, both_grads, sems = refs
    t = g_mine.shape[0]
    copies = start_fetch(wanted, me, tokens, grads, outs, sems)
    both_grads[:t] = g_mine[:, 512:]
    both_grads[t:] = g_theirs[:, 512:]

    def block(j, _):
        column = pl.multiple_of(j * 512, 512)
        both_tokens[:t] = mine[:, pl.ds(column, 512)]
        both_tokens[t:] = theirs[:, pl.ds(column, 512)]
        out[j] = lax.dot_general(
            both_tokens[...],
            both_grads[...],
            (((0,), (0,)), ((), ())),
            preferred_element_type=jnp.float32,
        )
        return _

    lax.fori_loop(0, out.shape[0], block, None)
    for copy in copies:
        copy.wait()


def product(me, tokens, grads, mine, theirs, g_mine, g_theirs, blocks, wanted, widths):
    t, k = g_mine.shape[0], 512
    vmem = pl.BlockSpec(memory_space=pltpu.VMEM)
    smem = pl.BlockSpec(memory_space=pltpu.SMEM)
    hbm = pl.BlockSpec(memory_space=pltpu.HBM)
    return pl.pallas_call(
        partial(product_kernel, wanted),
        in_specs=[smem, hbm, hbm] + [vmem] * 4,
        out_specs=[vmem] * (1 + len(wanted)),
        scratch_shapes=[
            pltpu.VMEM((2 * t, 512), mine.dtype),
            pltpu.VMEM((2 * t, k), mine.dtype),
            pltpu.SemaphoreType.DMA((8,)),
        ],
        out_shape=[pltpu.VMEM((blocks, 512, k), jnp.float32)]
        + [pltpu.VMEM((t, width), tokens.dtype) for width in widths],
        cost_estimate=pl.CostEstimate(
            flops=4 * t * 512 * blocks * k, bytes_accessed=4 * t * sum(widths), transcendentals=0
        ),
        compiler_params=pltpu.CompilerParams(vmem_limit_bytes=VMEM_LIMIT),
        name="product",
    )(
        me,
        pltpu.with_memory_space_constraint(tokens, pltpu.HBM),
        pltpu.with_memory_space_constraint(grads, pltpu.HBM),
        mine,
        theirs,
        g_mine,
        g_theirs,
    )


def squares_kernel(*refs):
    *pieces, out = refs
    total = sum(jnp.sum((p[...] * p[...]).reshape(-1, 8, 512), axis=0) for p in pieces)
    total = total[:, :128] + total[:, 128:256] + total[:, 256:384] + total[:, 384:]
    total = jnp.sum(total, axis=0, keepdims=True)
    out[...] = jnp.broadcast_to(total[None], out.shape)


def squares_of(pieces):
    return pl.pallas_call(
        squares_kernel,
        out_shape=jax.ShapeDtypeStruct((16, 1, 128), jnp.float32),
        compiler_params=pltpu.CompilerParams(vmem_limit_bytes=VMEM_LIMIT),
        name="squares",
    )(*pieces)


def adam_kernel(start, step_index, all_squares, *refs):
    *pieces, weights, first, second, updated, clip_out = refs
    squares = jnp.sum(all_squares[...], axis=0)
    squares = jnp.sum(squares, axis=1, keepdims=True)
    norm = jnp.sqrt(squares)
    clip = jnp.minimum(1.0, math.sqrt(8192 * 512) / (norm + NORM_EPS))
    clip_out[...] = jnp.broadcast_to(clip, clip_out.shape)
    steps = jnp.full((1, 1), step_index[0] + 1, jnp.int32).astype(jnp.float32)
    rate = LEARN_RATE / (1.0 - jnp.exp(steps * math.log(BETA_ONE)))
    second_scale = 1.0 / (1.0 - jnp.exp(steps * math.log(BETA_TWO)))
    row = start
    for piece in pieces:
        rows = pl.ds(row, piece.shape[0])
        mine = pl.ds(row - start, piece.shape[0])
        row += piece.shape[0]
        clipped = clip * piece[...]
        one = BETA_ONE * first[rows] + (1.0 - BETA_ONE) * clipped
        two = BETA_TWO * second[rows] + (1.0 - BETA_TWO) * clipped * clipped
        updated[mine] = weights[rows] - rate * one / (jnp.sqrt(two * second_scale) + ADAM_EPS)


def adam(start, step_index, all_squares, pieces, weights, first, second):
    vmem = pl.BlockSpec(memory_space=pltpu.VMEM)
    return pl.pallas_call(
        partial(adam_kernel, start),
        in_specs=[pl.BlockSpec(memory_space=pltpu.SMEM)] + [vmem] * (len(pieces) + 4),
        out_specs=[vmem] * 2,
        out_shape=[
            jax.ShapeDtypeStruct((sum(p.shape[0] for p in pieces), 512), jnp.float32),
            jax.ShapeDtypeStruct((8, 512), jnp.float32),
        ],
        cost_estimate=pl.CostEstimate(
            flops=20 * 512 * 512, bytes_accessed=16 * 512 * 512, transcendentals=512 * 512
        ),
        compiler_params=pltpu.CompilerParams(vmem_limit_bytes=VMEM_LIMIT),
        name="adam",
    )(step_index, all_squares, *pieces, weights, first, second)


def moments_kernel(clip, *refs):
    *pieces, first, second, new_first, new_second = refs
    row = 0
    for piece in pieces:
        rows = pl.ds(row, piece.shape[0])
        row += piece.shape[0]
        clipped = clip[:1] * piece[...]
        new_first[rows] = BETA_ONE * first[rows] + (1.0 - BETA_ONE) * clipped
        new_second[rows] = BETA_TWO * second[rows] + (1.0 - BETA_TWO) * clipped * clipped


def moments(clip, pieces, first, second):
    vmem = pl.BlockSpec(memory_space=pltpu.VMEM)
    return pl.pallas_call(
        moments_kernel,
        in_specs=[vmem] * (len(pieces) + 3),
        out_specs=[vmem] * 2,
        out_shape=[jax.ShapeDtypeStruct(first.shape, jnp.float32)] * 2,
        cost_estimate=pl.CostEstimate(
            flops=8 * first.size, bytes_accessed=20 * first.size, transcendentals=0
        ),
        compiler_params=pltpu.CompilerParams(vmem_limit_bytes=VMEM_LIMIT),
        name="moments",
    )(clip, *pieces, first, second)


def finish(apart, packed, updated, clip, pieces, weights, first, second, step_index, all_squares):
    f32 = jnp.float32
    start = packed.shape[0]
    if apart < 3:
        theirs = from_partner(apart, packed)
    behind, _ = adam(start, step_index, all_squares, pieces[1:], weights, first, second)
    packed_behind = behind.astype(jnp.float16)
    if apart < 3:
        theirs_behind = from_partner(apart, packed_behind)
    else:
        both = from_partner(apart, jnp.concatenate([packed, packed_behind]))
        theirs, theirs_behind = both[:start], both[start:]
    new_first, new_second = moments(clip, pieces, first, second)
    new_weights = jnp.concatenate(
        [0.5 * (updated + theirs.astype(f32)), 0.5 * (behind + theirs_behind.astype(f32))]
    )
    return new_weights, new_first, new_second


def local(tokens, key_grads, weights, first_moment, second_moment, step_index):
    inputs = tokens[0]
    grads_out = key_grads[0]
    me = lax.axis_index("fsdp")[None]

    source = (me, inputs, grads_out)
    (corner_out,) = fetch(me, inputs, grads_out, ((CORNER, 1),), (1024,))
    theirs_corner = exchange(corner_out, 0)
    far_out, mine_corner, mine_far = fetch(
        me, inputs, grads_out, ((FAR, 1), (CORNER, 0), (FAR, 0)), (1536, 1024, 1536)
    )
    theirs_far = exchange(far_out, 0)
    grads_pair = (mine_corner, theirs_corner)
    (acc_corner,) = product(*source, mine_corner, theirs_corner, *grads_pair, 1, (), ())

    def own(d, row, rows):
        acc, slot = (acc_far, FAR.index(d)) if d in FAR else (acc_near, NEAR.index(d))
        return acc[slot, row : row + rows]

    def pack(array, scale=1.0):
        return (array * scale).astype(jnp.float16)

    def unpack(message, scale):
        return message.astype(jnp.float32) * (1.0 / scale)

    parts = {dim: [p for at in range(3) for p in PARTS if p[2][at] == dim] for dim in (X, A, B)}
    packed = {}
    for dim in (X, A, B):
        row, rows, _ = parts[dim][0]
        packed[dim] = pack(acc_corner[0, row : row + rows], FIRST_SCALE)
    corner = {dim: exchange(packed[dim], dim) for dim in packed}
    mine_far, _ = lax.optimization_barrier((mine_far, packed))
    acc_far, near_out, mine_near = product(
        *source, mine_far, theirs_far, *grads_pair, 3, ((NEAR, 1), (NEAR, 0)), (2048, 2048)
    )
    theirs_near = exchange(near_out, 0)
    (acc_near,) = product(*source, mine_near, theirs_near, *grads_pair, 4, (), ())
    for dim in (X, A, B):
        row, rows, _ = parts[dim][0]
        packed[dim] = pack(acc_far[PAIR[dim][0], row : row + rows], FIRST_SCALE)
    pairs = {dim: exchange(packed[dim], dim) for dim in packed}

    def from_pair(dim, d):
        return unpack(pairs[dim][PAIR[dim][1].index(d)], FIRST_SCALE)

    for dim in (X, A, B):
        row, rows, (e1, e2, e3) = parts[dim][1]
        packed[dim] = pack(
            own(e2 | e3, row, rows) + unpack(corner[e1], FIRST_SCALE), SECOND_SCALE
        )
    ahead = {dim: exchange(packed[dim], dim) for dim in packed}
    for dim in (X, A, B):
        row, rows, _ = parts[dim][0]
        packed[dim] = pack(own(dim, row, rows), FIRST_SCALE)
    lasts = {dim: exchange(packed[dim], dim) for dim in packed}
    acc_near, _ = lax.optimization_barrier((acc_near, packed))
    for dim in (X, A, B):
        row, rows, (e1, e2, e3) = parts[dim][1]
        packed[dim] = pack(own(e2, row, rows) + from_pair(e1, e1 | e2), SECOND_SCALE)
    behinds = {dim: exchange(packed[dim], dim) for dim in packed}
    acc_near, _ = lax.optimization_barrier((acc_near, packed))
    for dim in (X, A, B):
        row, rows, (e1, e2, e3) = parts[dim][2]
        packed[dim] = pack(
            own(e3, row, rows) + from_pair(e1, e1 | e3) + unpack(ahead[e2], SECOND_SCALE),
            THIRD_SCALE,
        )
    thirds = {dim: exchange(packed[dim], dim) for dim in packed}
    acc_near, weights, first_moment, second_moment, _ = lax.optimization_barrier(
        (acc_near, weights[0], first_moment[0], second_moment[0], packed)
    )
    weights, first_moment, second_moment, level = hold(
        step_index, weights, first_moment, second_moment
    )
    acc_near, weights, first_moment, second_moment = lax.optimization_barrier(
        (acc_near, weights, first_moment, second_moment)
    )
    pieces = [
        own(0, row, rows)
        + unpack(lasts[e1], FIRST_SCALE)
        + unpack(behinds[e2], SECOND_SCALE)
        + unpack(thirds[e3], THIRD_SCALE)
        for row, rows, (e1, e2, e3) in PARTS
    ]

    all_squares = lax.all_to_all(squares_of(pieces), "fsdp", 0, 0, tiled=True)
    updated, clip = adam(
        0, step_index, all_squares, pieces[:1], weights, first_moment, second_moment
    )
    outs = conditionals._switch_internal(
        level[0],
        [partial(finish, apart) for apart in range(4)],
        (
            pack(updated),
            updated,
            clip,
            pieces,
            weights,
            first_moment,
            second_moment,
            step_index,
            all_squares,
        ),
        branches_platforms=None,
    )
    return tuple(out[None] for out in outs)


def solution(mesh):
    spec = P("replica", "fsdp", None)
    return jax.shard_map(
        local,
        mesh=mesh,
        in_specs=(spec, spec, spec, spec, spec, P()),
        out_specs=(spec, spec, spec),
        check_vma=False,
    )
```
